32 devices in a mesh: cam: 8 (over y, x, core), row: 4 (over z).
Axes of the slice: x: 2, y: 2, z: 4, core: 2. Of those that a mesh axis runs over, the one named last changes fastest.
Arguments:
- image: bfloat16 [8, 16, 128, 2048], P('cam', None, 'row'), may hold values from -6 to 6
- conv_first: bfloat16 [16, 144], replicated, may hold values from -0.5 to 0.5
- conv_second: bfloat16 [16, 144], replicated, may hold values from -0.5 to 0.5
- conv_uv: bfloat16 [16, 144], replicated, may hold values from -0.5 to 0.5
- send_block: int32 [8, 4, 32, 16], P('cam', 'row'), may hold values from 0 to 511
- send_shift: int32 [8, 4, 32, 16], P('cam', 'row'), may hold values from 0 to 127
- send_weight: int32 [8, 4, 32, 16], P('cam', 'row'), may hold values from 1 to 64
- send_count: int32 [8, 4, 32], P('cam', 'row'), may hold values from 0 to 16, as said below
- recv_tile: int32 [4, 8, 32, 16], P('row', 'cam'), may hold values from 0 to 1023
Outputs:
- texture: bfloat16 [16, 4096, 1024], P(None, 'row', 'cam')
The draws below stay inside these ranges and needn't reach their ends.
Inputs may be any that keep to these rules, and one draw needn't show every extreme that they name: `send_count`: slots of a list at or beyond its count are padding. In every draw one atlas region receives 16 used slots from every strip.
All inputs are finite; a program needn't handle non-finite values.
Results may differ from the reference program's by a relative error of at most 0.0066.
Values may be sent and summed in bfloat16 or wider, within the bound.
No kernel may reach another device: no remote copies, remote signals or barrier semaphores. Data moves between devices by JAX's collectives and lax.ppermute only.
A program may use at most 192 MiB of HBM per device.

```python
import jax
import jax.numpy as jnp
from jax import lax

C = 16
W = 2048
H_DEV = 32
TL = 128
CAP = 16
AR_DEV = 1024
CAMS = 8
STRIPS = 4
H = 128
NB = 512
AR = 4096
AC = 1024


def draw_send_count(key, part):
    key_pop = jax.random.fold_in(key, 11)
    key_raw = jax.random.fold_in(key, 12)
    key_full = jax.random.fold_in(key, 13)
    regions = CAMS * STRIPS
    popular = jax.random.randint(key_pop, (regions,), 2, 6)
    raw = jax.random.randint(key_raw, (CAMS, STRIPS, regions), 0, 1 << 20)
    raw = raw % (CAP * popular[None, None, :] // 4 + 1)
    counts = jnp.minimum(raw, CAP)
    full_region = jax.random.randint(key_full, (), 0, regions)
    target = lax.broadcasted_iota(jnp.int32, (CAMS, STRIPS, regions), 2)
    return jnp.where(target == full_region, CAP, counts).astype(jnp.int32)


def plant(drawn, stream_key, smallest, high):
    longest = drawn.shape.index(max(drawn.shape))
    spots = []
    for shift in (0, 1):
        where = [jax.random.randint(jax.random.fold_in(stream_key, axis), (), 0, length) for axis, length in enumerate(drawn.shape)]
        where[longest] = (where[longest] + shift) % drawn.shape[longest]
        spots.append(tuple(where))
    return drawn.at[spots[0]].set(smallest).at[spots[1]].set(high)


def level_of(own_key, extent, shards, smallest, top_value):
    loudness = 1.0
    for axis_at, parts in shards:
        draws = jax.random.uniform(jax.random.fold_in(jax.random.fold_in(own_key, 6), axis_at), (parts,), jnp.float32, smallest / len(shards), top_value / len(shards))
        loudness = loudness * jnp.repeat(jnp.exp(draws), extent[axis_at] // parts).reshape((-1,) + (1,) * (len(extent) - 1 - axis_at))
    return loudness


def gaussian(key, shape, spread, bound, cuts=(), kind=jnp.bfloat16):
    gain = level_of(key, shape, cuts, -0.22, 0.18) if cuts else 1.0
    array = jax.random.normal(key, shape, jnp.float32) * spread * gain
    return jnp.minimum(jnp.maximum(array, -bound), bound).astype(kind)


def setup_inputs(seed: int = 0) -> dict:
    streams_of = jax.random.split(jax.random.key(seed), 10)
    return {
        "image": gaussian(streams_of[0], (CAMS, C, H, W), 1.0, 6.0, ((0, 8), (2, 4))),
        "conv_first": gaussian(streams_of[1], (C, 9 * C), (9 * C) ** -0.5, 0.5),
        "conv_second": gaussian(streams_of[2], (C, 9 * C), (9 * C) ** -0.5, 0.5),
        "conv_uv": gaussian(streams_of[3], (C, 9 * C), (9 * C) ** -0.5, 0.5),
        "send_block": plant(jax.random.randint(streams_of[4], (CAMS, STRIPS, CAMS * STRIPS, CAP), 0, NB), jax.random.fold_in(streams_of[4], 1), 0, NB - 1).astype(jnp.int32),
        "send_shift": plant(jax.random.randint(streams_of[5], (CAMS, STRIPS, CAMS * STRIPS, CAP), 0, TL), jax.random.fold_in(streams_of[5], 1), 0, TL - 1).astype(jnp.int32),
        "send_weight": plant(jax.random.randint(streams_of[6], (CAMS, STRIPS, CAMS * STRIPS, CAP), 1, 65), jax.random.fold_in(streams_of[6], 1), 1, 64).astype(jnp.int32),
        "send_count": draw_send_count(jax.random.fold_in(streams_of[9], 71), 0),
        "recv_tile": plant(jax.random.randint(streams_of[8], (STRIPS, CAMS, CAMS * STRIPS, CAP), 0, AR_DEV), jax.random.fold_in(streams_of[8], 1), 0, AR_DEV - 1).astype(jnp.int32),
    }


def conv_layer(field, weight):
    channels = field.shape[0]
    height = field.shape[1]
    width = field.shape[2]
    padded = jnp.pad(field.astype(jnp.float32), ((0, 0), (1, 1), (1, 1)))
    kernel_all = weight.astype(jnp.float32)
    total = jnp.zeros((weight.shape[0], height, width), jnp.float32)
    for row_step in range(3):
        for col_step in range(3):
            offset = (row_step * 3 + col_step) * channels
            kernel = kernel_all[:, offset:offset + channels]
            window = padded[:, row_step:row_step + height, col_step:col_step + width]
            total = total + jnp.einsum("oi,ihw->ohw", kernel, window, precision=lax.Precision.HIGHEST)
    return total


def reference(image, conv_first, conv_second, conv_uv, send_block, send_shift, send_weight, send_count, recv_tile):
    def camera(pixels):
        hidden = jax.nn.silu(conv_layer(pixels, conv_first)).astype(jnp.bfloat16)
        return conv_layer(hidden, conv_second).astype(jnp.bfloat16)

    features = lax.map(camera, image)
    sources = CAMS * STRIPS
    per_row = W // TL
    blocks = features.reshape(CAMS, C, STRIPS, H_DEV, per_row, TL).transpose(0, 2, 3, 4, 1, 5).reshape(sources, NB, C, TL)
    flat_block = send_block.reshape(sources, sources, CAP)
    flat_shift = send_shift.reshape(sources, sources, CAP)
    flat_weight = send_weight.reshape(sources, sources, CAP)
    flat_count = send_count.reshape(sources, sources)
    flat_tile = recv_tile.transpose(1, 0, 2, 3).reshape(sources, sources, CAP)
    source_ids = jnp.arange(sources).astype(jnp.int32)
    slot_ids = jnp.arange(CAP).astype(jnp.int32)
    texel_ids = jnp.arange(TL).astype(jnp.int32)

    def owner(region):
        chosen = flat_block[:, region]
        shifts = flat_shift[:, region]
        counts = flat_count[:, region]
        values = blocks[source_ids[:, None], chosen]
        where_from = (texel_ids[None, None, :] - shifts[:, :, None]) % TL
        where_from = jnp.broadcast_to(where_from[:, :, None, :], values.shape).astype(jnp.int32)
        shifted = jnp.take_along_axis(values, where_from, axis=3)
        scales = jnp.where(slot_ids[None, :] < counts[:, None], flat_weight[:, region].astype(jnp.float32) / 16.0, jnp.float32(0.0))
        payload = (shifted.astype(jnp.float32) * scales[:, :, None, None]).astype(jnp.bfloat16)
        scale_wire = scales.astype(jnp.bfloat16)
        tiles = flat_tile[region].reshape(sources * CAP).astype(jnp.int32)
        total = jax.ops.segment_sum(payload.reshape(sources * CAP, C * TL).astype(jnp.float32), tiles, num_segments=AR_DEV)
        weight_sum = jax.ops.segment_sum(scale_wire.reshape(sources * CAP).astype(jnp.float32), tiles, num_segments=AR_DEV)
        joined = (total / jnp.maximum(weight_sum, jnp.float32(1.0))[:, None]).astype(jnp.bfloat16)
        return joined.reshape(AR_DEV, C, TL)

    regions = lax.map(owner, jnp.arange(sources).astype(jnp.int32))
    atlas = regions.reshape(CAMS, STRIPS, AR_DEV, C, TL).transpose(3, 1, 2, 0, 4).reshape(C, AR, AC)
    blended = atlas.astype(jnp.float32) + conv_layer(atlas, conv_uv)
    return blended.astype(jnp.bfloat16)
```

```python
import functools

import jax
import jax.numpy as jnp
from jax import lax
from jax.experimental import pallas as pl
from jax.experimental.pallas import tpu as pltpu
from jax.sharding import PartitionSpec as P

TL = 128
AR_DEV = 1024
GROUP = 8
VMEM_BYTES = 60 * 1024 * 1024
WHOLE = pl.BlockSpec(memory_space=pltpu.VMEM)
SCALARS = pl.BlockSpec(memory_space=pltpu.SMEM)


def neighbour(cells, axis, step):
    count = lax.axis_size(axis)
    pairs = [(i, i + step) for i in range(count) if 0 <= i + step < count]
    return lax.ppermute(cells, axis, pairs)


def band(weight, channel_major):
    tap_row = weight.shape[1] // 3
    rows = [
        jnp.pad(weight, ((0, 0), (tap_row * r, tap_row * (GROUP - 1 - r)))) for r in range(GROUP)
    ]
    stacked = jnp.stack(rows, axis=1 if channel_major else 0)
    return stacked.reshape(-1, stacked.shape[-1])


def lanes_of(shape):
    return lax.broadcasted_iota(jnp.int32, shape, len(shape) - 1)


def spread(row, lanes, taps_ref, cells):
    channels, width = cells.shape
    zero = jnp.zeros_like(cells)
    base = pl.multiple_of(row * (3 * channels), 3 * channels)
    taps_ref[pl.ds(base, channels), :] = jnp.where(lanes == 0, zero, pltpu.roll(cells, 1, 1))
    taps_ref[pl.ds(base + channels, channels), :] = cells
    taps_ref[pl.ds(base + 2 * channels, channels), :] = jnp.where(
        lanes == width - 1, zero, pltpu.roll(cells, width - 1, 1)
    )


def send_kernel(
    place_ref,
    block_ref,
    shift_ref,
    weight_ref,
    count_ref,
    image_ref,
    above_ref,
    below_ref,
    first_ref,
    second_ref,
    payload_ref,
    taps_ref,
    hidden_ref,
    feature_ref,
    slots_ref,
):
    rows, channels, width = image_ref.shape
    tap = 3 * channels
    reach = (GROUP + 2) * tap
    lanes = lanes_of((channels, width))
    for i in range(2):
        spread(i, lanes, taps_ref, above_ref[i])
        spread(rows + 2 + i, lanes, taps_ref, below_ref[i])

    @pl.loop(0, rows)
    def _(i):
        spread(i + 2, lanes, taps_ref, image_ref[i])

    step = 2 * TL
    has_above = (place_ref[0] > 0).astype(jnp.float32)
    has_below = (place_ref[0] < place_ref[1] - 1).astype(jnp.float32)

    @pl.loop(0, width // step)
    def _(j):
        cols = pl.ds(pl.multiple_of(j * step, step), step)

        def activate(v):
            return v / (1.0 + jnp.exp(-v))

        for g in range(rows // GROUP):
            window = taps_ref[pl.ds(g * GROUP * tap, reach), cols]
            out = activate(jnp.dot(first_ref[...], window, preferred_element_type=jnp.float32))
            out = out.reshape(GROUP, channels, step)
            if g == 0:
                out = jnp.concatenate([out[:1] * has_above, out[1:]], axis=0)
            hidden_ref[pl.ds(g * GROUP, GROUP), :, cols] = out.astype(jnp.bfloat16)
        window = taps_ref[pl.ds(rows * tap, 4 * tap), cols]
        out = activate(
            jnp.dot(
                first_ref[: 2 * channels, : 4 * tap], window, preferred_element_type=jnp.float32
            )
        ).reshape(2, channels, step)
        out = jnp.concatenate([out[:1], out[1:] * has_below], axis=0)
        hidden_ref[pl.ds(rows, 2), :, cols] = out.astype(jnp.bfloat16)

    @pl.loop(0, rows + 2)
    def _(i):
        spread(i, lanes, taps_ref, hidden_ref[i])

    per_row = width // TL

    @pl.loop(0, width // step)
    def _(j):
        cols = pl.ds(pl.multiple_of(j * step, step), step)
        for g in range(rows // GROUP):
            window = taps_ref[pl.ds(g * GROUP * tap, reach), cols]
            out = jnp.dot(second_ref[...], window, preferred_element_type=jnp.float32)
            out = out.astype(jnp.bfloat16).reshape(GROUP, channels, step)
            for r in range(GROUP):
                for half in range(2):
                    feature_ref[(g * GROUP + r) * per_row + 2 * j + half] = out[
                        r, :, half * TL : (half + 1) * TL
                    ]

    peers, capacity = block_ref.shape
    half = capacity // 2
    side = lanes_of((half, TL)) < TL // 2
    slot_row = lax.broadcasted_iota(jnp.int32, (half, TL), 0)

    @pl.loop(0, peers)
    def _(d):
        count = count_ref[0, d]
        factors = []
        for k in range(capacity):
            scale = jnp.where(k < count, weight_ref[d, k].astype(jnp.float32) * 0.0625, 0.0)
            factors.append(scale)
            cells = feature_ref[block_ref[d, k]].astype(jnp.float32)
            cells = pltpu.roll(cells, shift_ref[d, k], 1) * scale
            slots_ref[pl.ds(k, channels, stride=capacity), :] = cells
        payload_ref[d, : channels * capacity, :] = slots_ref[...].astype(jnp.bfloat16)
        record = jnp.zeros((half, TL), jnp.float32)
        for k in range(half):
            record = jnp.where(
                slot_row == k, jnp.where(side, factors[k], factors[k + half]), record
            )
        payload_ref[d, channels * capacity :, :] = record.astype(jnp.bfloat16)


def join_kernel(
    tile_ref, incoming_ref, joined_ref, first_ref, last_ref, onehot_ref, inverse_ref, cells_ref
):
    peers = incoming_ref.shape[0]
    entries = tile_ref.shape[1]
    capacity = entries // peers
    half = capacity // 2
    tiles = onehot_ref.shape[0]
    channels = joined_ref.shape[0] // tiles
    rows = 128

    @pl.loop(0, tiles // rows)
    def _(i):
        base = pl.multiple_of(i * rows, rows)
        ids = lax.broadcasted_iota(jnp.int32, (rows, entries), 0) + base
        onehot_ref[pl.ds(base, rows), :] = jnp.where(ids == tile_ref[...], 1.0, 0.0).astype(
            jnp.bfloat16
        )

    record = incoming_ref[:, channels * capacity :, :].astype(jnp.float32)
    record = record.reshape(peers * half, TL)
    other = pltpu.roll(record, TL // 2, 1)
    side = lanes_of(record.shape) < TL // 2
    low = jnp.where(side, record, other).reshape(peers, half, TL)
    high = jnp.where(side, other, record).reshape(peers, half, TL)
    scales = jnp.concatenate([low, high], axis=1).reshape(entries, TL).astype(jnp.bfloat16)
    total = jnp.dot(onehot_ref[...], scales, preferred_element_type=jnp.float32)
    inverse_ref[...] = 1.0 / jnp.maximum(total, 1.0)
    for q in range(0, channels, 2):
        pair = jnp.concatenate(
            [
                incoming_ref[:, p * capacity : (p + 1) * capacity, :].reshape(entries, TL)
                for p in (q, q + 1)
            ],
            axis=1,
        )
        total = jnp.dot(onehot_ref[...], pair, preferred_element_type=jnp.float32)
        for p in range(2):
            cells_ref[pl.ds(q + p, tiles, stride=channels), :] = (
                total[:, p * TL : (p + 1) * TL] * inverse_ref[...]
            )
    lanes = lanes_of((channels, TL))
    unroll = 8

    @pl.loop(0, tiles // TL)
    def _(i):
        def one(s, carry):
            left, right = carry
            for u in range(unroll):
                base = pl.multiple_of(((i * (TL // unroll) + s) * unroll + u) * channels, channels)
                cells = cells_ref[pl.ds(base, channels), :].astype(jnp.bfloat16)
                joined_ref[pl.ds(base, channels), :] = cells
                back = pltpu.roll(cells, TL - 1, 1)
                left = jnp.where(lanes == TL - 1, back, pltpu.roll(left, TL - 1, 1))
                right = jnp.where(lanes == TL - 1, cells, pltpu.roll(right, TL - 1, 1))
            return left, right

        zero = jnp.zeros((channels, TL), jnp.bfloat16)
        left, right = lax.fori_loop(0, TL // unroll, one, (zero, zero))
        cols = pl.ds(pl.multiple_of(i * TL, TL), TL)
        first_ref[:, cols] = left
        last_ref[:, cols] = right


def texture_kernel(
    joined_ref, above_ref, below_ref, before_ref, after_ref, weight_ref, residual_ref, texture_ref, taps_ref
):
    channels = texture_ref.shape[0]
    tiles = texture_ref.shape[1]
    tap = 3 * channels
    reach = (GROUP + 2) * tap
    lanes = lanes_of((channels, TL))

    def place(row, cells, before, after):
        base = pl.multiple_of(row * tap, channels)
        taps_ref[pl.ds(base, channels), :] = jnp.where(lanes == 0, before, pltpu.roll(cells, 1, 1))
        taps_ref[pl.ds(base + channels, channels), :] = cells
        taps_ref[pl.ds(base + 2 * channels, channels), :] = jnp.where(
            lanes == TL - 1, after, pltpu.roll(cells, TL - 1, 1)
        )

    def corner(ref, k, back):
        cells = ref[:, tiles + k * TL : tiles + (k + 1) * TL]
        return pltpu.roll(cells, 1 if back else TL - 1, 1)

    place(0, above_ref[...], corner(before_ref, 0, True), corner(after_ref, 0, False))
    place(tiles + 1, below_ref[...], corner(before_ref, 1, True), corner(after_ref, 1, False))
    unroll = 8

    @pl.loop(0, tiles // TL)
    def _(i):
        cols = pl.ds(pl.multiple_of(i * TL, TL), TL)

        def one(s, carry):
            before, after = carry
            for u in range(unroll):
                t = (i * (TL // unroll) + s) * unroll + u
                cells = joined_ref[pl.ds(pl.multiple_of(t * channels, channels), channels), :]
                place(t + 1, cells, before, after)
                before = pltpu.roll(before, TL - 1, 1)
                after = pltpu.roll(after, TL - 1, 1)
            return before, after

        lax.fori_loop(
            0, TL // unroll, one, (before_ref[:, cols], pltpu.roll(after_ref[:, cols], TL - 1, 1))
        )

    pair = 2 * GROUP

    @pl.loop(0, tiles // pair)
    def _(i):
        base = pl.multiple_of(i * (pair * tap), pair * tap)
        window = jnp.concatenate(
            [
                taps_ref[pl.ds(base, reach), :],
                taps_ref[pl.ds(base + GROUP * tap, reach), :],
            ],
            axis=1,
        )
        rows = pl.multiple_of(i * (pair * channels), pair * channels)
        own = jnp.concatenate(
            [
                joined_ref[pl.ds(rows, GROUP * channels), :],
                joined_ref[pl.ds(rows + GROUP * channels, GROUP * channels), :],
            ],
            axis=1,
        )
        out = jnp.dot(weight_ref[...], window, preferred_element_type=jnp.float32)
        out = out + jnp.dot(residual_ref[...], own, preferred_element_type=jnp.float32)
        out = out.reshape(channels, GROUP, 2 * TL)
        out = jnp.concatenate([out[:, :, :TL], out[:, :, TL:]], axis=1)
        texture_ref[:, pl.ds(pl.multiple_of(i * pair, pair), pair), :] = out.astype(jnp.bfloat16)


def call(kernel, outs, scratch, specs):
    return pl.pallas_call(
        kernel,
        out_shape=outs,
        in_specs=specs,
        out_specs=jax.tree.map(lambda _: WHOLE, outs),
        scratch_shapes=scratch,
        compiler_params=pltpu.CompilerParams(vmem_limit_bytes=VMEM_BYTES),
    )


def local(
    image,
    conv_first,
    conv_second,
    conv_uv,
    send_block,
    send_shift,
    send_weight,
    send_count,
    recv_tile,
):
    half = jnp.bfloat16
    pixels = image[0]
    channels, strip_rows, width = pixels.shape
    by_row = pixels.transpose(1, 0, 2)
    above = neighbour(by_row[-2:], "row", 1)
    below = neighbour(by_row[:2], "row", -1)
    place = jnp.stack([lax.axis_index("row"), lax.axis_size("row")]).astype(jnp.int32)
    peers, capacity = send_block.shape[2:]
    entries = peers * capacity
    message = channels * capacity + capacity // 2
    payload = call(
        send_kernel,
        jax.ShapeDtypeStruct((peers, message, TL), half),
        [
            pltpu.VMEM(((strip_rows + 4) * 3 * channels, width), half),
            pltpu.VMEM((strip_rows + 2, channels, width), half),
            pltpu.VMEM((strip_rows * width // TL, channels, TL), half),
            pltpu.VMEM((channels * capacity, TL), jnp.float32),
        ],
        [SCALARS] * 5 + [WHOLE] * 5,
    )(
        place,
        send_block[0, 0],
        send_shift[0, 0],
        send_weight[0, 0],
        send_count[0],
        by_row,
        above,
        below,
        band(conv_first, False),
        band(conv_second, False),
    )
    arrived = lax.all_to_all(payload, ("cam", "row"), split_axis=0, concat_axis=0, tiled=True)
    joined, first, last = call(
        join_kernel,
        (
            jax.ShapeDtypeStruct((AR_DEV * channels, TL), half),
            jax.ShapeDtypeStruct((channels, AR_DEV), half),
            jax.ShapeDtypeStruct((channels, AR_DEV), half),
        ),
        [
            pltpu.VMEM((AR_DEV, entries), half),
            pltpu.VMEM((AR_DEV, TL), jnp.float32),
            pltpu.VMEM((AR_DEV * channels, TL), jnp.float32),
        ],
        [WHOLE] * 2,
    )(recv_tile.reshape(1, entries), arrived)
    top = neighbour(joined[-channels:], "row", 1)
    bottom = neighbour(joined[:channels], "row", -1)
    before = neighbour(jnp.concatenate([last, top, bottom], axis=1), "cam", 1)
    after = neighbour(jnp.concatenate([first, top, bottom], axis=1), "cam", -1)
    same = (
        lax.broadcasted_iota(jnp.int32, (channels, GROUP, GROUP, channels), 0)
        == lax.broadcasted_iota(jnp.int32, (channels, GROUP, GROUP, channels), 3)
    ) & (
        lax.broadcasted_iota(jnp.int32, (channels, GROUP, GROUP, channels), 1)
        == lax.broadcasted_iota(jnp.int32, (channels, GROUP, GROUP, channels), 2)
    )
    residual = same.astype(half).reshape(channels * GROUP, GROUP * channels)
    return call(
        texture_kernel,
        jax.ShapeDtypeStruct((channels, AR_DEV, TL), half),
        [pltpu.VMEM(((AR_DEV + 2) * 3 * channels, TL), half)],
        [WHOLE] * 7,
    )(joined, top, bottom, before, after, band(conv_uv, True), residual)


def solution(mesh):
    return jax.shard_map(
        local,
        mesh=mesh,
        in_specs=(
            P("cam", None, "row", None),
            P(),
            P(),
            P(),
            P("cam", "row", None, None),
            P("cam", "row", None, None),
            P("cam", "row", None, None),
            P("cam", "row", None),
            P("row", "cam", None, None),
        ),
        out_specs=P(None, "row", "cam"),
        check_vma=False,
    )
```

```python
import functools

import jax
import jax.numpy as jnp
from jax import lax
from jax.experimental import pallas as pl
from jax.experimental.pallas import tpu as pltpu
from jax.sharding import PartitionSpec as P

TL = 128
AR_DEV = 1024
GROUP = 8
VMEM_BYTES = 60 * 1024 * 1024
WHOLE = pl.BlockSpec(memory_space=pltpu.VMEM)
SCALARS = pl.BlockSpec(memory_space=pltpu.SMEM)


def neighbour(cells, axis, step):
    count = lax.axis_size(axis)
    pairs = [(i, i + step) for i in range(count) if 0 <= i + step < count]
    return lax.ppermute(cells, axis, pairs)


def band(weight, channel_major):
    tap_row = weight.shape[1] // 3
    rows = [
        jnp.pad(weight, ((0, 0), (tap_row * r, tap_row * (GROUP - 1 - r)))) for r in range(GROUP)
    ]
    stacked = jnp.stack(rows, axis=1 if channel_major else 0)
    return stacked.reshape(-1, stacked.shape[-1])


def turn(cells, amount):
    return pltpu.roll(cells, lax.rem(amount, TL), 1)


def lanes_of(shape):
    return lax.broadcasted_iota(jnp.int32, shape, len(shape) - 1)


def spread(row, lanes, taps_ref, cells):
    channels, width = cells.shape
    zero = jnp.zeros_like(cells)
    base = pl.multiple_of(row * (3 * channels), 3 * channels)
    taps_ref[pl.ds(base, channels), :] = jnp.where(lanes == 0, zero, pltpu.roll(cells, 1, 1))
    taps_ref[pl.ds(base + channels, channels), :] = cells
    taps_ref[pl.ds(base + 2 * channels, channels), :] = jnp.where(
        lanes == width - 1, zero, pltpu.roll(cells, width - 1, 1)
    )


def send_kernel(
    place_ref,
    block_ref,
    shift_ref,
    weight_ref,
    count_ref,
    image_ref,
    above_ref,
    below_ref,
    first_ref,
    second_ref,
    payload_ref,
    taps_ref,
    hidden_ref,
    feature_ref,
    slots_ref,
):
    rows, channels, width = image_ref.shape
    tap = 3 * channels
    reach = (GROUP + 2) * tap
    lanes = lanes_of((channels, width))
    for i in range(2):
        spread(i, lanes, taps_ref, above_ref[i])
        spread(rows + 2 + i, lanes, taps_ref, below_ref[i])

    @pl.loop(0, rows)
    def _(i):
        spread(i + 2, lanes, taps_ref, image_ref[i])

    step = 2 * TL
    has_above = (place_ref[0] > 0).astype(jnp.float32)
    has_below = (place_ref[0] < place_ref[1] - 1).astype(jnp.float32)

    @pl.loop(0, width // step)
    def _(j):
        cols = pl.ds(pl.multiple_of(j * step, step), step)

        def activate(v):
            return v / (1.0 + jnp.exp(-v))

        for g in range(rows // GROUP):
            window = taps_ref[pl.ds(g * GROUP * tap, reach), cols]
            out = activate(jnp.dot(first_ref[...], window, preferred_element_type=jnp.float32))
            out = out.reshape(GROUP, channels, step)
            if g == 0:
                out = jnp.concatenate([out[:1] * has_above, out[1:]], axis=0)
            hidden_ref[pl.ds(g * GROUP, GROUP), :, cols] = out.astype(jnp.bfloat16)
        window = taps_ref[pl.ds(rows * tap, 4 * tap), cols]
        out = activate(
            jnp.dot(
                first_ref[: 2 * channels, : 4 * tap], window, preferred_element_type=jnp.float32
            )
        ).reshape(2, channels, step)
        out = jnp.concatenate([out[:1], out[1:] * has_below], axis=0)
        hidden_ref[pl.ds(rows, 2), :, cols] = out.astype(jnp.bfloat16)

    @pl.loop(0, rows + 2)
    def _(i):
        spread(i, lanes, taps_ref, hidden_ref[i])

    per_row = width // TL

    @pl.loop(0, width // step)
    def _(j):
        cols = pl.ds(pl.multiple_of(j * step, step), step)
        for g in range(rows // GROUP):
            window = taps_ref[pl.ds(g * GROUP * tap, reach), cols]
            out = jnp.dot(second_ref[...], window, preferred_element_type=jnp.float32)
            out = out.astype(jnp.bfloat16).reshape(GROUP, channels, step)
            for r in range(GROUP):
                for half in range(2):
                    feature_ref[(g * GROUP + r) * per_row + 2 * j + half] = out[
                        r, :, half * TL : (half + 1) * TL
                    ]

    peers, capacity = block_ref.shape
    half = capacity // 2
    side = lanes_of((half, TL)) < TL // 2
    slot_row = lax.broadcasted_iota(jnp.int32, (half, TL), 0)

    @pl.loop(0, peers)
    def _(d):
        count = count_ref[0, d]
        factors = []
        for k in range(capacity):
            scale = jnp.where(k < count, weight_ref[d, k].astype(jnp.float32) * 0.0625, 0.0)
            factors.append(scale)
            cells = feature_ref[block_ref[d, k]].astype(jnp.float32)
            cells = pltpu.roll(cells, shift_ref[d, k], 1) * scale
            slots_ref[pl.ds(k, channels, stride=capacity), :] = cells
        payload_ref[d, : channels * capacity, :] = slots_ref[...].astype(jnp.bfloat16)
        record = jnp.zeros((half, TL), jnp.float32)
        for k in range(half):
            record = jnp.where(
                slot_row == k, jnp.where(side, factors[k], factors[k + half]), record
            )
        payload_ref[d, channels * capacity :, :] = record.astype(jnp.bfloat16)


def join_kernel(
    tile_ref, incoming_ref, joined_ref, first_ref, last_ref, onehot_ref, inverse_ref, cells_ref
):
    peers = incoming_ref.shape[0]
    entries = tile_ref.shape[1]
    capacity = entries // peers
    half = capacity // 2
    tiles = onehot_ref.shape[0]
    channels = joined_ref.shape[0] // tiles
    rows = 128

    @pl.loop(0, tiles // rows)
    def _(i):
        base = pl.multiple_of(i * rows, rows)
        ids = lax.broadcasted_iota(jnp.int32, (rows, entries), 0) + base
        onehot_ref[pl.ds(base, rows), :] = jnp.where(ids == tile_ref[...], 1.0, 0.0).astype(
            jnp.bfloat16
        )

    record = incoming_ref[:, channels * capacity :, :].astype(jnp.float32)
    record = record.reshape(peers * half, TL)
    other = pltpu.roll(record, TL // 2, 1)
    side = lanes_of(record.shape) < TL // 2
    low = jnp.where(side, record, other).reshape(peers, half, TL)
    high = jnp.where(side, other, record).reshape(peers, half, TL)
    scales = jnp.concatenate([low, high], axis=1).reshape(entries, TL).astype(jnp.bfloat16)
    total = jnp.dot(onehot_ref[...], scales, preferred_element_type=jnp.float32)
    inverse_ref[...] = 1.0 / jnp.maximum(total, 1.0)
    for q in range(0, channels, 2):
        pair = jnp.concatenate(
            [
                incoming_ref[:, p * capacity : (p + 1) * capacity, :].reshape(entries, TL)
                for p in (q, q + 1)
            ],
            axis=1,
        )
        total = jnp.dot(onehot_ref[...], pair, preferred_element_type=jnp.float32)
        for p in range(2):
            cells_ref[pl.ds(q + p, tiles, stride=channels), :] = (
                total[:, p * TL : (p + 1) * TL] * inverse_ref[...]
            )
    lanes = lanes_of((channels, TL))
    unroll = 8

    @pl.loop(0, tiles // TL)
    def _(i):
        def one(s, carry):
            left, right = carry
            for u in range(unroll):
                t = s * unroll + u
                base = pl.multiple_of((i * TL + t) * channels, channels)
                cells = cells_ref[pl.ds(base, channels), :].astype(jnp.bfloat16)
                joined_ref[pl.ds(base, channels), :] = cells
                left = jnp.where(lanes == t, turn(cells, t), left)
                right = jnp.where(lanes == t, turn(cells, t + 1), right)
            return left, right

        zero = jnp.zeros((channels, TL), jnp.bfloat16)
        left, right = lax.fori_loop(0, TL // unroll, one, (zero, zero))
        cols = pl.ds(pl.multiple_of(i * TL, TL), TL)
        first_ref[:, cols] = left
        last_ref[:, cols] = right


def texture_kernel(
    joined_ref, above_ref, below_ref, before_ref, after_ref, weight_ref, residual_ref, texture_ref, taps_ref
):
    channels = texture_ref.shape[0]
    tiles = texture_ref.shape[1]
    tap = 3 * channels
    reach = (GROUP + 2) * tap
    lanes = lanes_of((channels, TL))

    def place(row, cells, before, after):
        base = pl.multiple_of(row * tap, channels)
        taps_ref[pl.ds(base, channels), :] = jnp.where(lanes == 0, before, pltpu.roll(cells, 1, 1))
        taps_ref[pl.ds(base + channels, channels), :] = cells
        taps_ref[pl.ds(base + 2 * channels, channels), :] = jnp.where(
            lanes == TL - 1, after, pltpu.roll(cells, TL - 1, 1)
        )

    def corner(ref, k, back):
        cells = ref[:, tiles + k * TL : tiles + (k + 1) * TL]
        return pltpu.roll(cells, 1 if back else TL - 1, 1)

    place(0, above_ref[...], corner(before_ref, 0, True), corner(after_ref, 0, False))
    place(tiles + 1, below_ref[...], corner(before_ref, 1, True), corner(after_ref, 1, False))
    unroll = 8

    @pl.loop(0, tiles // TL)
    def _(i):
        cols = pl.ds(pl.multiple_of(i * TL, TL), TL)

        before = before_ref[:, cols]
        after = after_ref[:, cols]

        @pl.loop(0, TL // unroll)
        def _(s):
            for u in range(unroll):
                t = s * unroll + u
                row = i * TL + t
                cells = joined_ref[pl.ds(pl.multiple_of(row * channels, channels), channels), :]
                place(row + 1, cells, turn(before, TL - t), turn(after, TL - 1 - t))

    pair = 2 * GROUP

    @pl.loop(0, tiles // pair)
    def _(i):
        base = pl.multiple_of(i * (pair * tap), pair * tap)
        window = jnp.concatenate(
            [
                taps_ref[pl.ds(base, reach), :],
                taps_ref[pl.ds(base + GROUP * tap, reach), :],
            ],
            axis=1,
        )
        rows = pl.multiple_of(i * (pair * channels), pair * channels)
        own = jnp.concatenate(
            [
                joined_ref[pl.ds(rows, GROUP * channels), :],
                joined_ref[pl.ds(rows + GROUP * channels, GROUP * channels), :],
            ],
            axis=1,
        )
        out = jnp.dot(weight_ref[...], window, preferred_element_type=jnp.float32)
        out = out + jnp.dot(residual_ref[...], own, preferred_element_type=jnp.float32)
        out = out.reshape(channels, GROUP, 2 * TL)
        out = jnp.concatenate([out[:, :, :TL], out[:, :, TL:]], axis=1)
        texture_ref[:, pl.ds(pl.multiple_of(i * pair, pair), pair), :] = out.astype(jnp.bfloat16)


def call(kernel, outs, scratch, specs):
    return pl.pallas_call(
        kernel,
        out_shape=outs,
        in_specs=specs,
        out_specs=jax.tree.map(lambda _: WHOLE, outs),
        scratch_shapes=scratch,
        compiler_params=pltpu.CompilerParams(vmem_limit_bytes=VMEM_BYTES),
    )


def local(
    image,
    conv_first,
    conv_second,
    conv_uv,
    send_block,
    send_shift,
    send_weight,
    send_count,
    recv_tile,
):
    half = jnp.bfloat16
    pixels = image[0]
    channels, strip_rows, width = pixels.shape
    by_row = pixels.transpose(1, 0, 2)
    above = neighbour(by_row[-2:], "row", 1)
    below = neighbour(by_row[:2], "row", -1)
    place = jnp.stack([lax.axis_index("row"), lax.axis_size("row")]).astype(jnp.int32)
    peers, capacity = send_block.shape[2:]
    entries = peers * capacity
    message = channels * capacity + capacity // 2
    payload = call(
        send_kernel,
        jax.ShapeDtypeStruct((peers, message, TL), half),
        [
            pltpu.VMEM(((strip_rows + 4) * 3 * channels, width), half),
            pltpu.VMEM((strip_rows + 2, channels, width), half),
            pltpu.VMEM((strip_rows * width // TL, channels, TL), half),
            pltpu.VMEM((channels * capacity, TL), jnp.float32),
        ],
        [SCALARS] * 5 + [WHOLE] * 5,
    )(
        place,
        send_block[0, 0],
        send_shift[0, 0],
        send_weight[0, 0],
        send_count[0],
        by_row,
        above,
        below,
        band(conv_first, False),
        band(conv_second, False),
    )
    arrived = lax.all_to_all(payload, ("cam", "row"), split_axis=0, concat_axis=0, tiled=True)
    joined, first, last = call(
        join_kernel,
        (
            jax.ShapeDtypeStruct((AR_DEV * channels, TL), half),
            jax.ShapeDtypeStruct((channels, AR_DEV), half),
            jax.ShapeDtypeStruct((channels, AR_DEV), half),
        ),
        [
            pltpu.VMEM((AR_DEV, entries), half),
            pltpu.VMEM((AR_DEV, TL), jnp.float32),
            pltpu.VMEM((AR_DEV * channels, TL), jnp.float32),
        ],
        [WHOLE] * 2,
    )(recv_tile.reshape(1, entries), arrived)
    top = neighbour(joined[-channels:], "row", 1)
    bottom = neighbour(joined[:channels], "row", -1)
    before = neighbour(jnp.concatenate([last, top, bottom], axis=1), "cam", 1)
    after = neighbour(jnp.concatenate([first, top, bottom], axis=1), "cam", -1)
    same = (
        lax.broadcasted_iota(jnp.int32, (channels, GROUP, GROUP, channels), 0)
        == lax.broadcasted_iota(jnp.int32, (channels, GROUP, GROUP, channels), 3)
    ) & (
        lax.broadcasted_iota(jnp.int32, (channels, GROUP, GROUP, channels), 1)
        == lax.broadcasted_iota(jnp.int32, (channels, GROUP, GROUP, channels), 2)
    )
    residual = same.astype(half).reshape(channels * GROUP, GROUP * channels)
    return call(
        texture_kernel,
        jax.ShapeDtypeStruct((channels, AR_DEV, TL), half),
        [pltpu.VMEM(((AR_DEV + 2) * 3 * channels, TL), half)],
        [WHOLE] * 7,
    )(joined, top, bottom, before, after, band(conv_uv, True), residual)


def solution(mesh):
    return jax.shard_map(
        local,
        mesh=mesh,
        in_specs=(
            P("cam", None, "row", None),
            P(),
            P(),
            P(),
            P("cam", "row", None, None),
            P("cam", "row", None, None),
            P("cam", "row", None, None),
            P("cam", "row", None),
            P("row", "cam", None, None),
        ),
        out_specs=P(None, "row", "cam"),
        check_vma=False,
    )
```

```python
import jax
import jax.numpy as jnp
from jax import lax
from jax.experimental import pallas as pl
from jax.experimental.pallas import tpu as pltpu
from jax.sharding import PartitionSpec as P

TL = 128
AR_DEV = 1024
GROUP = 8
VMEM_BYTES = 60 * 1024 * 1024
WHOLE = pl.BlockSpec(memory_space=pltpu.VMEM)
SCALARS = pl.BlockSpec(memory_space=pltpu.SMEM)


def neighbour(cells, axis, step):
    count = lax.axis_size(axis)
    pairs = [(i, i + step) for i in range(count) if 0 <= i + step < count]
    return lax.ppermute(cells, axis, pairs)


def band(weight, channel_major):
    tap_row = weight.shape[1] // 3
    rows = [
        jnp.pad(weight, ((0, 0), (tap_row * r, tap_row * (GROUP - 1 - r)))) for r in range(GROUP)
    ]
    stacked = jnp.stack(rows, axis=1 if channel_major else 0)
    return stacked.reshape(-1, stacked.shape[-1])


def turn(cells, amount):
    return pltpu.roll(cells, lax.rem(amount, TL), 1)


def lanes_of(shape):
    return lax.broadcasted_iota(jnp.int32, shape, len(shape) - 1)


def spread(row, lanes, taps_ref, cells):
    channels, width = cells.shape
    zero = jnp.zeros_like(cells)
    base = pl.multiple_of(row * (3 * channels), 3 * channels)
    taps_ref[pl.ds(base, channels), :] = jnp.where(lanes == 0, zero, pltpu.roll(cells, 1, 1))
    taps_ref[pl.ds(base + channels, channels), :] = cells
    taps_ref[pl.ds(base + 2 * channels, channels), :] = jnp.where(
        lanes == width - 1, zero, pltpu.roll(cells, width - 1, 1)
    )


def send_kernel(
    place_ref,
    block_ref,
    shift_ref,
    weight_ref,
    count_ref,
    image_ref,
    above_ref,
    below_ref,
    first_ref,
    second_ref,
    payload_ref,
    taps_ref,
    hidden_ref,
    feature_ref,
    slots_ref,
):
    rows, channels, width = image_ref.shape
    tap = 3 * channels
    reach = (GROUP + 2) * tap
    lanes = lanes_of((channels, width))
    for i in range(2):
        spread(i, lanes, taps_ref, above_ref[i])
        spread(rows + 2 + i, lanes, taps_ref, below_ref[i])

    @pl.loop(0, rows)
    def _(i):
        spread(i + 2, lanes, taps_ref, image_ref[i])

    step = 2 * TL
    has_above = (place_ref[0] > 0).astype(jnp.float32)
    has_below = (place_ref[0] < place_ref[1] - 1).astype(jnp.float32)

    @pl.loop(0, width // step)
    def _(j):
        cols = pl.ds(pl.multiple_of(j * step, step), step)

        def activate(v):
            return v / (1.0 + jnp.exp(-v))

        for g in range(rows // GROUP):
            window = taps_ref[pl.ds(g * GROUP * tap, reach), cols]
            out = activate(jnp.dot(first_ref[...], window, preferred_element_type=jnp.float32))
            out = out.reshape(GROUP, channels, step)
            if g == 0:
                out = jnp.concatenate([out[:1] * has_above, out[1:]], axis=0)
            hidden_ref[pl.ds(g * GROUP, GROUP), :, cols] = out.astype(jnp.bfloat16)
        window = taps_ref[pl.ds(rows * tap, 4 * tap), cols]
        out = activate(
            jnp.dot(
                first_ref[: 2 * channels, : 4 * tap], window, preferred_element_type=jnp.float32
            )
        ).reshape(2, channels, step)
        out = jnp.concatenate([out[:1], out[1:] * has_below], axis=0)
        hidden_ref[pl.ds(rows, 2), :, cols] = out.astype(jnp.bfloat16)

    @pl.loop(0, rows + 2)
    def _(i):
        spread(i, lanes, taps_ref, hidden_ref[i])

    per_row = width // TL

    @pl.loop(0, width // step)
    def _(j):
        cols = pl.ds(pl.multiple_of(j * step, step), step)
        for g in range(rows // GROUP):
            window = taps_ref[pl.ds(g * GROUP * tap, reach), cols]
            out = jnp.dot(second_ref[...], window, preferred_element_type=jnp.float32)
            out = out.astype(jnp.bfloat16).reshape(GROUP, channels, step)
            for r in range(GROUP):
                for half in range(2):
                    feature_ref[(g * GROUP + r) * per_row + 2 * j + half] = out[
                        r, :, half * TL : (half + 1) * TL
                    ]

    peers, capacity = block_ref.shape
    half = capacity // 2
    side = lanes_of((half, TL)) < TL // 2
    slot_row = lax.broadcasted_iota(jnp.int32, (half, TL), 0)

    @pl.loop(0, peers)
    def _(d):
        count = count_ref[0, d]
        factors = []
        for k in range(capacity):
            scale = jnp.where(k < count, weight_ref[d, k].astype(jnp.float32) * 0.0625, 0.0)
            factors.append(scale)
            cells = feature_ref[block_ref[d, k]].astype(jnp.float32)
            cells = pltpu.roll(cells, shift_ref[d, k], 1) * scale
            slots_ref[pl.ds(k, channels, stride=capacity), :] = cells
        payload_ref[d, : channels * capacity, :] = slots_ref[...].astype(jnp.bfloat16)
        record = jnp.zeros((half, TL), jnp.float32)
        for k in range(half):
            record = jnp.where(
                slot_row == k, jnp.where(side, factors[k], factors[k + half]), record
            )
        payload_ref[d, channels * capacity :, :] = record.astype(jnp.bfloat16)


def join_kernel(
    tile_ref, incoming_ref, joined_ref, first_ref, last_ref, onehot_ref, inverse_ref, cells_ref
):
    peers = incoming_ref.shape[0]
    entries = tile_ref.shape[1]
    capacity = entries // peers
    half = capacity // 2
    tiles = onehot_ref.shape[0]
    channels = joined_ref.shape[0] // tiles
    rows = 128

    @pl.loop(0, tiles // rows)
    def _(i):
        base = pl.multiple_of(i * rows, rows)
        ids = lax.broadcasted_iota(jnp.int32, (rows, entries), 0) + base
        onehot_ref[pl.ds(base, rows), :] = jnp.where(ids == tile_ref[...], 1.0, 0.0).astype(
            jnp.bfloat16
        )

    record = incoming_ref[:, channels * capacity :, :].astype(jnp.float32)
    record = record.reshape(peers * half, TL)
    other = pltpu.roll(record, TL // 2, 1)
    side = lanes_of(record.shape) < TL // 2
    low = jnp.where(side, record, other).reshape(peers, half, TL)
    high = jnp.where(side, other, record).reshape(peers, half, TL)
    scales = jnp.concatenate([low, high], axis=1).reshape(entries, TL).astype(jnp.bfloat16)
    total = jnp.dot(onehot_ref[...], scales, preferred_element_type=jnp.float32)
    inverse_ref[...] = 1.0 / jnp.maximum(total, 1.0)
    for q in range(0, channels, 2):
        pair = jnp.concatenate(
            [
                incoming_ref[:, p * capacity : (p + 1) * capacity, :].reshape(entries, TL)
                for p in (q, q + 1)
            ],
            axis=1,
        )
        total = jnp.dot(onehot_ref[...], pair, preferred_element_type=jnp.float32)
        for p in range(2):
            cells_ref[pl.ds(q + p, tiles, stride=channels), :] = (
                total[:, p * TL : (p + 1) * TL] * inverse_ref[...]
            )
    lanes = lanes_of((channels, TL))
    unroll = 8

    @pl.loop(0, tiles // TL)
    def _(i):
        def one(s, carry):
            left, right = carry
            for u in range(unroll):
                t = s * unroll + u
                base = pl.multiple_of((i * TL + t) * channels, channels)
                cells = cells_ref[pl.ds(base, channels), :].astype(jnp.bfloat16)
                joined_ref[pl.ds(base, channels), :] = cells
                left = jnp.where(lanes == t, turn(cells, t), left)
                right = jnp.where(lanes == t, turn(cells, t + 1), right)
            return left, right

        zero = jnp.zeros((channels, TL), jnp.bfloat16)
        left, right = lax.fori_loop(0, TL // unroll, one, (zero, zero))
        cols = pl.ds(pl.multiple_of(i * TL, TL), TL)
        first_ref[:, cols] = left
        last_ref[:, cols] = right


def texture_kernel(
    joined_ref, prev_ref, next_ref, above_ref, below_ref, before_ref, after_ref, weight_ref, residual_ref,
    texture_ref, even_ref, odd_ref
):
    channels = texture_ref.shape[0]
    step = pl.program_id(0)
    blocks = pl.num_programs(0) - 1
    tap = 3 * channels
    reach = (GROUP + 2) * tap
    lanes = lanes_of((channels, TL))
    tiles = blocks * TL

    def place(taps_ref, row, cells, before, after):
        base = row * tap
        taps_ref[base : base + channels, :] = jnp.where(lanes == 0, before, pltpu.roll(cells, 1, 1))
        taps_ref[base + channels : base + 2 * channels, :] = cells
        taps_ref[base + 2 * channels : base + 3 * channels, :] = jnp.where(
            lanes == TL - 1, after, pltpu.roll(cells, TL - 1, 1)
        )

    def fill(taps_ref):
        i = jnp.minimum(step, blocks - 1)
        here = pl.ds(pl.multiple_of(i * TL, TL), TL)
        first = pl.ds(pl.multiple_of(jnp.where(i == 0, tiles, (i - 1) * TL), TL), TL)
        last = pl.ds(pl.multiple_of(jnp.where(i == blocks - 1, tiles + TL, (i + 1) * TL), TL), TL)
        cells = jnp.where(i == 0, above_ref[...], prev_ref[...])
        place(taps_ref, 0, cells, pltpu.roll(before_ref[:, first], 1, 1), after_ref[:, first])
        cells = jnp.where(i == blocks - 1, below_ref[...], next_ref[...])
        place(taps_ref, TL + 1, cells, before_ref[:, last], pltpu.roll(after_ref[:, last], TL - 1, 1))
        before = before_ref[:, here]
        after = after_ref[:, here]
        for t in range(TL):
            cells = joined_ref[t * channels : (t + 1) * channels, :]
            place(taps_ref, t + 1, cells, pltpu.roll(before, (TL - t) % TL, 1), pltpu.roll(after, TL - 1 - t, 1))

    def convolve(taps_ref):
        pair = 2 * GROUP
        for i in range(TL // pair):
            base = i * pair * tap
            window = jnp.concatenate(
                [taps_ref[base + h * GROUP * tap : base + h * GROUP * tap + reach, :] for h in range(2)], axis=1
            )
            out = jnp.dot(weight_ref[...], window, preferred_element_type=jnp.float32)
            own = jnp.concatenate(
                [
                    jnp.concatenate(
                        [
                            taps_ref[base + (h * GROUP + r + 1) * tap + channels : base + (h * GROUP + r + 1) * tap + 2 * channels, :]
                            for r in range(GROUP)
                        ],
                        axis=0,
                    )
                    for h in range(2)
                ],
                axis=1,
            )
            out = out + jnp.dot(residual_ref[...], own, preferred_element_type=jnp.float32)
            out = out.reshape(channels, GROUP, 2 * TL)
            out = jnp.concatenate([out[:, :, :TL], out[:, :, TL:]], axis=1)
            texture_ref[:, i * pair : (i + 1) * pair, :] = out.astype(jnp.bfloat16)

    @pl.when(lax.rem(step, 2) == 0)
    def _():
        fill(even_ref)
        convolve(odd_ref)

    @pl.when(lax.rem(step, 2) == 1)
    def _():
        fill(odd_ref)
        convolve(even_ref)


def texture_call(joined, above, below, before, after, weight, residual):
    channels = above.shape[0]
    tiles = joined.shape[0] // channels
    blocks = tiles // TL
    def at(i):
        return jnp.minimum(i, blocks - 1)
    whole = lambda x: pl.BlockSpec(x.shape, lambda i: (0,) * x.ndim)
    return pl.pallas_call(
        texture_kernel,
        grid=(blocks + 1,),
        out_shape=jax.ShapeDtypeStruct((channels, tiles, TL), jnp.bfloat16),
        in_specs=[
            pl.BlockSpec((TL * channels, TL), lambda i: (at(i), 0)),
            pl.BlockSpec((channels, TL), lambda i: (jnp.maximum(at(i) * TL - 1, 0), 0)),
            pl.BlockSpec((channels, TL), lambda i: (jnp.minimum((at(i) + 1) * TL, tiles - 1), 0)),
        ] + [whole(x) for x in (above, below, before, after, weight, residual)],
        out_specs=pl.BlockSpec((channels, TL, TL), lambda i: (0, jnp.maximum(i - 1, 0), 0)),
        scratch_shapes=[pltpu.VMEM(((TL + 2) * 3 * channels, TL), jnp.bfloat16)] * 2,
        compiler_params=pltpu.CompilerParams(vmem_limit_bytes=VMEM_BYTES),
    )(joined, joined, joined, above, below, before, after, weight, residual)


def call(kernel, outs, scratch, specs):
    return pl.pallas_call(
        kernel,
        out_shape=outs,
        in_specs=specs,
        out_specs=jax.tree.map(lambda _: WHOLE, outs),
        scratch_shapes=scratch,
        compiler_params=pltpu.CompilerParams(vmem_limit_bytes=VMEM_BYTES),
    )


def local(
    image,
    conv_first,
    conv_second,
    conv_uv,
    send_block,
    send_shift,
    send_weight,
    send_count,
    recv_tile,
):
    half = jnp.bfloat16
    pixels = image[0]
    channels, strip_rows, width = pixels.shape
    by_row = pixels.transpose(1, 0, 2)
    above = neighbour(by_row[-2:], "row", 1)
    below = neighbour(by_row[:2], "row", -1)
    place = jnp.stack([lax.axis_index("row"), lax.axis_size("row")]).astype(jnp.int32)
    peers, capacity = send_block.shape[2:]
    entries = peers * capacity
    message = channels * capacity + capacity // 2
    payload = call(
        send_kernel,
        jax.ShapeDtypeStruct((peers, message, TL), half),
        [
            pltpu.VMEM(((strip_rows + 4) * 3 * channels, width), half),
            pltpu.VMEM((strip_rows + 2, channels, width), half),
            pltpu.VMEM((strip_rows * width // TL, channels, TL), half),
            pltpu.VMEM((channels * capacity, TL), jnp.float32),
        ],
        [SCALARS] * 5 + [WHOLE] * 5,
    )(
        place,
        send_block[0, 0],
        send_shift[0, 0],
        send_weight[0, 0],
        send_count[0],
        by_row,
        above,
        below,
        band(conv_first, False),
        band(conv_second, False),
    )
    arrived = lax.all_to_all(payload, ("cam", "row"), split_axis=0, concat_axis=0, tiled=True)
    joined, first, last = call(
        join_kernel,
        (
            jax.ShapeDtypeStruct((AR_DEV * channels, TL), half),
            jax.ShapeDtypeStruct((channels, AR_DEV), half),
            jax.ShapeDtypeStruct((channels, AR_DEV), half),
        ),
        [
            pltpu.VMEM((AR_DEV, entries), half),
            pltpu.VMEM((AR_DEV, TL), jnp.float32),
            pltpu.VMEM((AR_DEV * channels, TL), jnp.float32),
        ],
        [WHOLE] * 2,
    )(recv_tile.reshape(1, entries), arrived)
    top = neighbour(joined[-channels:], "row", 1)
    bottom = neighbour(joined[:channels], "row", -1)
    before = neighbour(jnp.concatenate([last, top, jnp.roll(bottom, 1, 1)], axis=1), "cam", 1)
    after = neighbour(jnp.concatenate([first, jnp.roll(top, -1, 1), bottom], axis=1), "cam", -1)
    same = (
        lax.broadcasted_iota(jnp.int32, (channels, GROUP, GROUP, channels), 0)
        == lax.broadcasted_iota(jnp.int32, (channels, GROUP, GROUP, channels), 3)
    ) & (
        lax.broadcasted_iota(jnp.int32, (channels, GROUP, GROUP, channels), 1)
        == lax.broadcasted_iota(jnp.int32, (channels, GROUP, GROUP, channels), 2)
    )
    residual = same.astype(half).reshape(channels * GROUP, GROUP * channels)
    return texture_call(joined, top, bottom, before, after, band(conv_uv, True), residual)


def solution(mesh):
    return jax.shard_map(
        local,
        mesh=mesh,
        in_specs=(
            P("cam", None, "row", None),
            P(),
            P(),
            P(),
            P("cam", "row", None, None),
            P("cam", "row", None, None),
            P("cam", "row", None, None),
            P("cam", "row", None),
            P("row", "cam", None, None),
        ),
        out_specs=P(None, "row", "cam"),
        check_vma=False,
    )
```

```python
import jax
import jax.numpy as jnp
from jax import lax
from jax.experimental import pallas as pl
from jax.experimental.pallas import tpu as pltpu
from jax.sharding import PartitionSpec as P

TL = 128
AR_DEV = 1024
GROUP = 8
SHIFT_BIT = 16
WEIGHT_BIT = 23
VMEM_BYTES = 60 * 1024 * 1024
WHOLE = pl.BlockSpec(memory_space=pltpu.VMEM)
SCALARS = pl.BlockSpec(memory_space=pltpu.SMEM)


def neighbour(cells, axis, step):
    count = lax.axis_size(axis)
    pairs = [(i, i + step) for i in range(count) if 0 <= i + step < count]
    return lax.ppermute(cells, axis, pairs)


def band(weight, channel_major):
    tap_row = weight.shape[1] // 3
    rows = [
        jnp.pad(weight, ((0, 0), (tap_row * r, tap_row * (GROUP - 1 - r)))) for r in range(GROUP)
    ]
    stacked = jnp.stack(rows, axis=1 if channel_major else 0)
    return stacked.reshape(-1, stacked.shape[-1])


def lanes_of(shape):
    return lax.broadcasted_iota(jnp.int32, shape, len(shape) - 1)


def spread(row, lanes, taps_ref, cells):
    channels, width = cells.shape
    zero = jnp.zeros_like(cells)
    base = pl.multiple_of(row * (3 * channels), 3 * channels)
    taps_ref[pl.ds(base, channels), :] = jnp.where(lanes == 0, zero, pltpu.roll(cells, 1, 1))
    taps_ref[pl.ds(base + channels, channels), :] = cells
    taps_ref[pl.ds(base + 2 * channels, channels), :] = jnp.where(
        lanes == width - 1, zero, pltpu.roll(cells, width - 1, 1)
    )


def send_kernel(
    place_ref,
    slot_ref,
    image_ref,
    above_ref,
    below_ref,
    first_ref,
    second_ref,
    payload_ref,
    taps_ref,
    hidden_ref,
    feature_ref,
    slots_ref,
):
    rows, channels, width = image_ref.shape
    tap = 3 * channels
    reach = (GROUP + 2) * tap
    lanes = lanes_of((channels, width))
    for i in range(2):
        spread(i, lanes, taps_ref, above_ref[i])
        spread(rows + 2 + i, lanes, taps_ref, below_ref[i])

    @pl.loop(0, rows)
    def _(i):
        spread(i + 2, lanes, taps_ref, image_ref[i])

    step = 2 * TL
    has_above = (place_ref[0] > 0).astype(jnp.float32)
    has_below = (place_ref[0] < place_ref[1] - 1).astype(jnp.float32)

    @pl.loop(0, width // step)
    def _(j):
        cols = pl.ds(pl.multiple_of(j * step, step), step)

        def activate(v):
            return v / (1.0 + jnp.exp(-v))

        for g in range(rows // GROUP):
            window = taps_ref[pl.ds(g * GROUP * tap, reach), cols]
            out = activate(jnp.dot(first_ref[...], window, preferred_element_type=jnp.float32))
            out = out.reshape(GROUP, channels, step)
            if g == 0:
                out = jnp.concatenate([out[:1] * has_above, out[1:]], axis=0)
            hidden_ref[pl.ds(g * GROUP, GROUP), :, cols] = out.astype(jnp.bfloat16)
        window = taps_ref[pl.ds(rows * tap, 4 * tap), cols]
        out = activate(
            jnp.dot(
                first_ref[: 2 * channels, : 4 * tap], window, preferred_element_type=jnp.float32
            )
        ).reshape(2, channels, step)
        out = jnp.concatenate([out[:1], out[1:] * has_below], axis=0)
        hidden_ref[pl.ds(rows, 2), :, cols] = out.astype(jnp.bfloat16)

    @pl.loop(0, rows + 2)
    def _(i):
        spread(i, lanes, taps_ref, hidden_ref[i])

    per_row = width // TL

    @pl.loop(0, width // step)
    def _(j):
        cols = pl.ds(pl.multiple_of(j * step, step), step)
        for g in range(rows // GROUP):
            window = taps_ref[pl.ds(g * GROUP * tap, reach), cols]
            out = jnp.dot(second_ref[...], window, preferred_element_type=jnp.float32)
            out = out.astype(jnp.bfloat16).reshape(GROUP, channels, step)
            for r in range(GROUP):
                for half in range(2):
                    feature_ref[(g * GROUP + r) * per_row + 2 * j + half] = out[
                        r, :, half * TL : (half + 1) * TL
                    ]

    peers, capacity = slot_ref.shape
    half = capacity // 2
    side = lanes_of((half, TL)) < TL // 2
    slot_row = lax.broadcasted_iota(jnp.int32, (half, TL), 0)

    @pl.loop(0, peers)
    def _(d):
        record = jnp.zeros((half, TL), jnp.float32)
        for k in range(capacity):
            slot = slot_ref[d, k]
            scale = lax.shift_right_logical(slot, WEIGHT_BIT).astype(jnp.float32) * 0.0625
            cells = feature_ref[slot & ((1 << SHIFT_BIT) - 1)]
            shift = lax.shift_right_logical(slot, SHIFT_BIT) & (TL - 1)
            cells = pltpu.roll(cells, shift, 1).astype(jnp.float32) * scale
            slots_ref[pl.ds(k, channels, stride=capacity), :] = cells
            here = (slot_row == k % half) & (side == (k < half))
            record = jnp.where(here, scale, record)
        payload_ref[d, : channels * capacity, :] = slots_ref[...].astype(jnp.bfloat16)
        payload_ref[d, channels * capacity :, :] = record.astype(jnp.bfloat16)


def scales_of(incoming_ref, entries):
    peers, message, lanes = incoming_ref.shape
    capacity = entries // peers
    half = capacity // 2
    record = incoming_ref[:, message - half :, :].astype(jnp.float32).reshape(peers * half, lanes)
    other = pltpu.roll(record, lanes // 2, 1)
    side = lanes_of(record.shape) < lanes // 2
    low = jnp.where(side, record, other).reshape(peers, half, lanes)
    high = jnp.where(side, other, record).reshape(peers, half, lanes)
    return jnp.concatenate([low, high], axis=1).reshape(entries, lanes).astype(jnp.bfloat16)


def join_kernel(tile_ref, incoming_ref, joined_ref, edge_ref, cells_ref, scales_ref):
    peers = incoming_ref.shape[0]
    entries = tile_ref.shape[1]
    capacity = entries // peers
    channels = edge_ref.shape[0]

    @pl.when(pl.program_id(0) == 0)
    def _():
        scales_ref[...] = scales_of(incoming_ref, entries)

    ids = lax.broadcasted_iota(jnp.int32, (TL, entries), 0) + pl.program_id(0) * TL
    onehot = jnp.where(ids == tile_ref[...], 1.0, 0.0).astype(jnp.bfloat16)
    total = jnp.dot(onehot, scales_ref[...], preferred_element_type=jnp.float32)
    inverse = 1.0 / jnp.maximum(total, 1.0)
    for q in range(0, channels, 2):
        pair = jnp.concatenate(
            [
                incoming_ref[:, p * capacity : (p + 1) * capacity, :].reshape(entries, TL)
                for p in (q, q + 1)
            ],
            axis=1,
        )
        total = jnp.dot(onehot, pair, preferred_element_type=jnp.float32)
        for p in range(2):
            cells_ref[pl.ds(q + p, TL, stride=channels), :] = (
                total[:, p * TL : (p + 1) * TL] * inverse
            )
    lanes = lanes_of((channels, TL))
    for part in range(2):
        edge = jnp.zeros((channels, TL), jnp.bfloat16)
        for u in range(TL // 2):
            base = (part * (TL // 2) + u) * channels
            cells = cells_ref[base : base + channels, :].astype(jnp.bfloat16)
            joined_ref[base : base + channels, :] = cells
            edge = jnp.where(lanes // 2 == u, pltpu.roll(cells, 2 * u + 1, 1), edge)
        edge_ref[:, part * TL : (part + 1) * TL] = edge


def join_call(tiles, incoming, channels):
    half = jnp.bfloat16
    entries = tiles.shape[1]
    return pl.pallas_call(
        join_kernel,
        grid=(AR_DEV // TL,),
        out_shape=(
            jax.ShapeDtypeStruct((AR_DEV * channels, TL), half),
            jax.ShapeDtypeStruct((channels, 2 * AR_DEV), half),
        ),
        in_specs=[
            pl.BlockSpec(tiles.shape, lambda i: (0, 0)),
            pl.BlockSpec(incoming.shape, lambda i: (0, 0, 0)),
        ],
        out_specs=(
            pl.BlockSpec((TL * channels, TL), lambda i: (i, 0)),
            pl.BlockSpec((channels, 2 * TL), lambda i: (0, i)),
        ),
        scratch_shapes=[
            pltpu.VMEM((TL * channels, TL), jnp.float32),
            pltpu.VMEM((entries, TL), half),
        ],
        compiler_params=pltpu.CompilerParams(vmem_limit_bytes=VMEM_BYTES),
    )(tiles, incoming)


def texture_kernel(
    joined_ref, prev_ref, next_ref, above_ref, below_ref, before_ref, after_ref, weight_ref, residual_ref,
    texture_ref, even_ref, odd_ref
):
    channels = texture_ref.shape[0]
    step = pl.program_id(0)
    blocks = pl.num_programs(0) - 1
    tap = 3 * channels
    reach = (GROUP + 2) * tap
    lanes = lanes_of((channels, TL))
    tiles = blocks * TL

    def place(taps_ref, row, cells, edge):
        base = row * tap
        taps_ref[base : base + channels, :] = jnp.where(lanes == 0, edge, pltpu.roll(cells, 1, 1))
        taps_ref[base + channels : base + 2 * channels, :] = cells
        taps_ref[base + 2 * channels : base + 3 * channels, :] = jnp.where(
            lanes == TL - 1, edge, pltpu.roll(cells, TL - 1, 1)
        )

    odd = lanes % 2 == 1

    def edges(before, after, before_lane, after_lane):
        return jnp.where(
            lanes == TL - 1,
            pltpu.roll(after, TL - 1 - after_lane, 1),
            pltpu.roll(before, TL - before_lane, 1),
        )

    def fill(taps_ref):
        i = jnp.minimum(step, blocks - 1)

        def both(part):
            cols = pl.ds(pl.multiple_of(part * TL, TL), TL)
            return before_ref[:, cols], after_ref[:, cols]

        outer = edges(*both(2 * blocks), TL - 1, 0)
        inner = edges(*both(jnp.maximum(2 * i - 1, 0)), TL - 2, TL - 1)
        place(
            taps_ref,
            0,
            jnp.where(i == 0, above_ref[...], prev_ref[...]),
            jnp.where(i == 0, outer, inner),
        )
        outer = edges(*both(2 * blocks + 1), TL - 1, 0)
        inner = edges(*both(jnp.minimum(2 * i + 2, 2 * blocks - 1)), 0, 1)
        place(
            taps_ref,
            TL + 1,
            jnp.where(i == blocks - 1, below_ref[...], next_ref[...]),
            jnp.where(i == blocks - 1, outer, inner),
        )
        for part in range(2):
            before, after = both(2 * i + part)
            merged = jnp.where(odd, after, pltpu.roll(before, 2, 1))
            for u in range(TL // 2):
                t = part * (TL // 2) + u
                cells = joined_ref[t * channels : (t + 1) * channels, :]
                place(taps_ref, t + 1, cells, pltpu.roll(merged, TL - 2 - 2 * u, 1))

    def convolve(taps_ref):
        pair = 2 * GROUP
        for i in range(TL // pair):
            base = i * pair * tap
            window = jnp.concatenate(
                [taps_ref[base + h * GROUP * tap : base + h * GROUP * tap + reach, :] for h in range(2)], axis=1
            )
            out = jnp.dot(weight_ref[...], window, preferred_element_type=jnp.float32)
            own = jnp.concatenate(
                [
                    jnp.concatenate(
                        [
                            taps_ref[base + (h * GROUP + r + 1) * tap + channels : base + (h * GROUP + r + 1) * tap + 2 * channels, :]
                            for r in range(GROUP)
                        ],
                        axis=0,
                    )
                    for h in range(2)
                ],
                axis=1,
            )
            out = out + jnp.dot(residual_ref[...], own, preferred_element_type=jnp.float32)
            out = out.reshape(channels, GROUP, 2 * TL)
            out = jnp.concatenate([out[:, :, :TL], out[:, :, TL:]], axis=1)
            texture_ref[:, i * pair : (i + 1) * pair, :] = out.astype(jnp.bfloat16)

    @pl.when(lax.rem(step, 2) == 0)
    def _():
        fill(even_ref)
        convolve(odd_ref)

    @pl.when(lax.rem(step, 2) == 1)
    def _():
        fill(odd_ref)
        convolve(even_ref)


def texture_call(joined, above, below, before, after, weight, residual):
    channels = above.shape[0]
    tiles = joined.shape[0] // channels
    blocks = tiles // TL
    def at(i):
        return jnp.minimum(i, blocks - 1)
    whole = lambda x: pl.BlockSpec(x.shape, lambda i: (0,) * x.ndim)
    return pl.pallas_call(
        texture_kernel,
        grid=(blocks + 1,),
        out_shape=jax.ShapeDtypeStruct((channels, tiles, TL), jnp.bfloat16),
        in_specs=[
            pl.BlockSpec((TL * channels, TL), lambda i: (at(i), 0)),
            pl.BlockSpec((channels, TL), lambda i: (jnp.maximum(at(i) * TL - 1, 0), 0)),
            pl.BlockSpec((channels, TL), lambda i: (jnp.minimum((at(i) + 1) * TL, tiles - 1), 0)),
        ] + [whole(x) for x in (above, below, before, after, weight, residual)],
        out_specs=pl.BlockSpec((channels, TL, TL), lambda i: (0, jnp.maximum(i - 1, 0), 0)),
        scratch_shapes=[pltpu.VMEM(((TL + 2) * 3 * channels, TL), jnp.bfloat16)] * 2,
        compiler_params=pltpu.CompilerParams(vmem_limit_bytes=VMEM_BYTES),
    )(joined, joined, joined, above, below, before, after, weight, residual)


def call(kernel, outs, scratch, specs):
    return pl.pallas_call(
        kernel,
        out_shape=outs,
        in_specs=specs,
        out_specs=jax.tree.map(lambda _: WHOLE, outs),
        scratch_shapes=scratch,
        compiler_params=pltpu.CompilerParams(vmem_limit_bytes=VMEM_BYTES),
    )


def local(
    image,
    conv_first,
    conv_second,
    conv_uv,
    send_block,
    send_shift,
    send_weight,
    send_count,
    recv_tile,
):
    half = jnp.bfloat16
    pixels = image[0]
    channels, strip_rows, width = pixels.shape
    by_row = pixels.transpose(1, 0, 2)
    above = neighbour(by_row[-2:], "row", 1)
    below = neighbour(by_row[:2], "row", -1)
    place = jnp.stack([lax.axis_index("row"), lax.axis_size("row")]).astype(jnp.int32)
    peers, capacity = send_block.shape[2:]
    entries = peers * capacity
    message = channels * capacity + capacity // 2
    used = lax.broadcasted_iota(jnp.int32, (peers, capacity), 1) < send_count.reshape(peers, 1)
    slots = (
        send_block[0, 0]
        + (send_shift[0, 0] << SHIFT_BIT)
        + (jnp.where(used, send_weight[0, 0], 0) << WEIGHT_BIT)
    )
    payload = call(
        send_kernel,
        jax.ShapeDtypeStruct((peers, message, TL), half),
        [
            pltpu.VMEM(((strip_rows + 4) * 3 * channels, width), half),
            pltpu.VMEM((strip_rows + 2, channels, width), half),
            pltpu.VMEM((strip_rows * width // TL, channels, TL), half),
            pltpu.VMEM((channels * capacity, TL), jnp.float32),
        ],
        [SCALARS] * 2 + [WHOLE] * 5,
    )(place, slots, by_row, above, below, band(conv_first, False), band(conv_second, False))
    arrived = lax.all_to_all(payload, ("cam", "row"), split_axis=0, concat_axis=0, tiled=True)
    joined, edge = join_call(recv_tile.reshape(1, entries), arrived, channels)
    top = neighbour(joined[-channels:], "row", 1)
    bottom = neighbour(joined[:channels], "row", -1)
    rim = jnp.concatenate([edge, top, bottom], axis=1)
    before = neighbour(rim, "cam", 1)
    after = neighbour(rim, "cam", -1)
    same = (
        lax.broadcasted_iota(jnp.int32, (channels, GROUP, GROUP, channels), 0)
        == lax.broadcasted_iota(jnp.int32, (channels, GROUP, GROUP, channels), 3)
    ) & (
        lax.broadcasted_iota(jnp.int32, (channels, GROUP, GROUP, channels), 1)
        == lax.broadcasted_iota(jnp.int32, (channels, GROUP, GROUP, channels), 2)
    )
    residual = same.astype(half).reshape(channels * GROUP, GROUP * channels)
    return texture_call(joined, top, bottom, before, after, band(conv_uv, True), residual)


def solution(mesh):
    return jax.shard_map(
        local,
        mesh=mesh,
        in_specs=(
            P("cam", None, "row", None),
            P(),
            P(),
            P(),
            P("cam", "row", None, None),
            P("cam", "row", None, None),
            P("cam", "row", None, None),
            P("cam", "row", None),
            P("row", "cam", None, None),
        ),
        out_specs=P(None, "row", "cam"),
        check_vma=False,
    )
```

```python
import jax
import jax.numpy as jnp
from jax import lax
from jax.experimental import pallas as pl
from jax.experimental.pallas import tpu as pltpu
from jax.sharding import PartitionSpec as P

TL = 128
AR_DEV = 1024
GROUP = 8
SHIFT_BIT = 16
WEIGHT_BIT = 23
VMEM_BYTES = 32 * 1024 * 1024
WHOLE = pl.BlockSpec(memory_space=pltpu.VMEM)
SCALARS = pl.BlockSpec(memory_space=pltpu.SMEM)


def swap(even_pairs, odd_pairs, axis):
    count = lax.axis_size(axis)
    received = []
    for start, cells in enumerate((even_pairs, odd_pairs)):
        pairs = [(i, i + 1) for i in range(start, count - 1, 2)]
        received.append(lax.ppermute(cells, axis, pairs + [(j, i) for i, j in pairs]))
    return received


def ordered(odd, even_pairs, odd_pairs):
    return jnp.where(odd, even_pairs, odd_pairs), jnp.where(odd, odd_pairs, even_pairs)


def band(weight, channel_major):
    tap_row = weight.shape[1] // 3
    rows = [
        jnp.pad(weight, ((0, 0), (tap_row * r, tap_row * (GROUP - 1 - r)))) for r in range(GROUP)
    ]
    stacked = jnp.stack(rows, axis=1 if channel_major else 0)
    return stacked.reshape(-1, stacked.shape[-1])


def lanes_of(shape):
    return lax.broadcasted_iota(jnp.int32, shape, len(shape) - 1)


def spread(row, lanes, taps_ref, cells):
    channels, width = cells.shape
    zero = jnp.zeros_like(cells)
    base = pl.multiple_of(row * (3 * channels), 3 * channels)
    taps_ref[pl.ds(base, channels), :] = jnp.where(lanes == 0, zero, pltpu.roll(cells, 1, 1))
    taps_ref[pl.ds(base + channels, channels), :] = cells
    taps_ref[pl.ds(base + 2 * channels, channels), :] = jnp.where(
        lanes == width - 1, zero, pltpu.roll(cells, width - 1, 1)
    )


def send_kernel(
    place_ref,
    slot_ref,
    image_ref,
    even_ref,
    odd_ref,
    first_ref,
    second_ref,
    payload_ref,
    taps_ref,
    hidden_ref,
    feature_ref,
    slots_ref,
):
    rows, channels, width = image_ref.shape
    tap = 3 * channels
    reach = (GROUP + 2) * tap
    lanes = lanes_of((channels, width))
    odd = place_ref[0] % 2 == 1
    for i in range(2):
        above, below = ordered(odd, even_ref[i], odd_ref[i])
        spread(i, lanes, taps_ref, above)
        spread(rows + 2 + i, lanes, taps_ref, below)

    @pl.loop(0, rows)
    def _(i):
        spread(i + 2, lanes, taps_ref, image_ref[i])

    step = 2 * TL
    has_above = (place_ref[0] > 0).astype(jnp.float32)
    has_below = (place_ref[0] < place_ref[1] - 1).astype(jnp.float32)

    @pl.loop(0, width // step)
    def _(j):
        cols = pl.ds(pl.multiple_of(j * step, step), step)

        def activate(v):
            return v / (1.0 + jnp.exp(-v))

        for g in range(rows // GROUP):
            window = taps_ref[pl.ds(g * GROUP * tap, reach), cols]
            out = activate(jnp.dot(first_ref[...], window, preferred_element_type=jnp.float32))
            out = out.reshape(GROUP, channels, step)
            if g == 0:
                out = jnp.concatenate([out[:1] * has_above, out[1:]], axis=0)
            hidden_ref[pl.ds(g * GROUP, GROUP), :, cols] = out.astype(jnp.bfloat16)
        window = taps_ref[pl.ds(rows * tap, 4 * tap), cols]
        out = activate(
            jnp.dot(
                first_ref[: 2 * channels, : 4 * tap], window, preferred_element_type=jnp.float32
            )
        ).reshape(2, channels, step)
        out = jnp.concatenate([out[:1], out[1:] * has_below], axis=0)
        hidden_ref[pl.ds(rows, 2), :, cols] = out.astype(jnp.bfloat16)

    @pl.loop(0, rows + 2)
    def _(i):
        spread(i, lanes, taps_ref, hidden_ref[i])

    per_row = width // TL

    @pl.loop(0, width // step)
    def _(j):
        cols = pl.ds(pl.multiple_of(j * step, step), step)
        for g in range(rows // GROUP):
            window = taps_ref[pl.ds(g * GROUP * tap, reach), cols]
            out = jnp.dot(second_ref[...], window, preferred_element_type=jnp.float32)
            out = out.astype(jnp.bfloat16).reshape(GROUP, channels, step)
            for r in range(GROUP):
                for half in range(2):
                    feature_ref[(g * GROUP + r) * per_row + 2 * j + half] = out[
                        r, :, half * TL : (half + 1) * TL
                    ]

    peers, capacity = slot_ref.shape
    half = capacity // 2
    side = lanes_of((half, TL)) < TL // 2
    slot_row = lax.broadcasted_iota(jnp.int32, (half, TL), 0)

    @pl.loop(0, peers)
    def _(d):
        record = jnp.zeros((half, TL), jnp.float32)
        for k in range(capacity):
            slot = slot_ref[d, k]
            scale = lax.shift_right_logical(slot, WEIGHT_BIT).astype(jnp.float32) * 0.0625
            cells = feature_ref[slot & ((1 << SHIFT_BIT) - 1)]
            shift = lax.shift_right_logical(slot, SHIFT_BIT) & (TL - 1)
            cells = pltpu.roll(cells, shift, 1).astype(jnp.float32) * scale
            slots_ref[pl.ds(k, channels, stride=capacity), :] = cells
            here = (slot_row == k % half) & (side == (k < half))
            record = jnp.where(here, scale, record)
        payload_ref[d, : channels * capacity, :] = slots_ref[...].astype(jnp.bfloat16)
        payload_ref[d, channels * capacity :, :] = record.astype(jnp.bfloat16)


def scales_of(incoming_ref, entries):
    peers, message, lanes = incoming_ref.shape
    capacity = entries // peers
    half = capacity // 2
    record = incoming_ref[:, message - half :, :].astype(jnp.float32).reshape(peers * half, lanes)
    other = pltpu.roll(record, lanes // 2, 1)
    side = lanes_of(record.shape) < lanes // 2
    low = jnp.where(side, record, other).reshape(peers, half, lanes)
    high = jnp.where(side, other, record).reshape(peers, half, lanes)
    return jnp.concatenate([low, high], axis=1).reshape(entries, lanes).astype(jnp.bfloat16)


def join_kernel(
    place_ref, tile_ref, incoming_ref, joined_ref, edge_ref, even_ref, odd_ref, cells_ref, scales_ref
):
    peers = incoming_ref.shape[0]
    entries = tile_ref.shape[1]
    capacity = entries // peers
    channels = edge_ref.shape[0]

    @pl.when(pl.program_id(0) == 0)
    def _():
        scales_ref[...] = scales_of(incoming_ref, entries)

    ids = lax.broadcasted_iota(jnp.int32, (TL, entries), 0) + pl.program_id(0) * TL
    onehot = jnp.where(ids == tile_ref[...], 1.0, 0.0).astype(jnp.bfloat16)
    total = jnp.dot(onehot, scales_ref[...], preferred_element_type=jnp.float32)
    inverse = 1.0 / jnp.maximum(total, 1.0)
    for q in range(0, channels, 2):
        pair = jnp.concatenate(
            [
                incoming_ref[:, p * capacity : (p + 1) * capacity, :].reshape(entries, TL)
                for p in (q, q + 1)
            ],
            axis=1,
        )
        total = jnp.dot(onehot, pair, preferred_element_type=jnp.float32)
        for p in range(2):
            cells_ref[pl.ds(q + p, TL, stride=channels), :] = (
                total[:, p * TL : (p + 1) * TL] * inverse
            )
    lanes = lanes_of((channels, TL))
    for part in range(2):
        edge = jnp.zeros((channels, TL), jnp.bfloat16)
        for u in range(TL // 2):
            base = (part * (TL // 2) + u) * channels
            cells = cells_ref[base : base + channels, :].astype(jnp.bfloat16)
            joined_ref[base : base + channels, :] = cells
            edge = jnp.where(lanes // 2 == u, pltpu.roll(cells, 2 * u + 1, 1), edge)
        edge_ref[:, part * TL : (part + 1) * TL] = edge

    step = pl.program_id(0)
    odd = place_ref[0] % 2
    head = joined_ref[:channels, :]
    tail = joined_ref[-channels:, :]

    @pl.when((step == 0) & (odd == 1))
    def _():
        even_ref[...] = head

    @pl.when((step == 0) & (odd == 0))
    def _():
        odd_ref[...] = head

    @pl.when((step == pl.num_programs(0) - 1) & (odd == 1))
    def _():
        odd_ref[...] = tail

    @pl.when((step == pl.num_programs(0) - 1) & (odd == 0))
    def _():
        even_ref[...] = tail


def join_call(place, tiles, incoming, channels):
    half = jnp.bfloat16
    entries = tiles.shape[1]
    return pl.pallas_call(
        join_kernel,
        grid=(AR_DEV // TL,),
        out_shape=(
            jax.ShapeDtypeStruct((AR_DEV * channels, TL), half),
            jax.ShapeDtypeStruct((channels, 2 * AR_DEV), half),
            jax.ShapeDtypeStruct((channels, TL), half),
            jax.ShapeDtypeStruct((channels, TL), half),
        ),
        in_specs=[
            SCALARS,
            pl.BlockSpec(tiles.shape, lambda i: (0, 0)),
            pl.BlockSpec(incoming.shape, lambda i: (0, 0, 0)),
        ],
        out_specs=(
            pl.BlockSpec((TL * channels, TL), lambda i: (i, 0)),
            pl.BlockSpec((channels, 2 * TL), lambda i: (0, i)),
            pl.BlockSpec((channels, TL), lambda i: (0, 0)),
            pl.BlockSpec((channels, TL), lambda i: (0, 0)),
        ),
        scratch_shapes=[
            pltpu.VMEM((TL * channels, TL), jnp.float32),
            pltpu.VMEM((entries, TL), half),
        ],
        compiler_params=pltpu.CompilerParams(vmem_limit_bytes=VMEM_BYTES),
    )(place, tiles, incoming)


def texture_kernel(
    place_ref,
    joined_ref,
    prev_ref,
    next_ref,
    even_end_ref,
    odd_end_ref,
    even_rim_ref,
    odd_rim_ref,
    weight_ref,
    residual_ref,
    texture_ref,
    even_ref,
    odd_ref,
):
    channels = texture_ref.shape[0]
    step = pl.program_id(0)
    blocks = pl.num_programs(0) - 1
    tap = 3 * channels
    reach = (GROUP + 2) * tap
    lanes = lanes_of((channels, TL))
    tiles = blocks * TL

    def place(taps_ref, row, cells, edge):
        base = row * tap
        taps_ref[base : base + channels, :] = jnp.where(lanes == 0, edge, pltpu.roll(cells, 1, 1))
        taps_ref[base + channels : base + 2 * channels, :] = cells
        taps_ref[base + 2 * channels : base + 3 * channels, :] = jnp.where(
            lanes == TL - 1, edge, pltpu.roll(cells, TL - 1, 1)
        )

    odd = lanes % 2 == 1

    def edges(before, after, before_lane, after_lane):
        return jnp.where(
            lanes == TL - 1,
            pltpu.roll(after, TL - 1 - after_lane, 1),
            pltpu.roll(before, TL - before_lane, 1),
        )

    def fill(taps_ref):
        i = jnp.minimum(step, blocks - 1)
        odd_row = place_ref[0] % 2
        odd_cam = place_ref[2] % 2 == 1
        above, below = ordered(odd_row == 1, even_end_ref[...], odd_end_ref[...])

        def both(part):
            cols = pl.ds(pl.multiple_of(part * TL, TL), TL)
            return ordered(odd_cam, even_rim_ref[:, cols], odd_rim_ref[:, cols])

        outer = edges(*both(2 * blocks + 1 - odd_row), TL - 1, 0)
        inner = edges(*both(jnp.maximum(2 * i - 1, 0)), TL - 2, TL - 1)
        place(
            taps_ref,
            0,
            jnp.where(i == 0, above, prev_ref[...]),
            jnp.where(i == 0, outer, inner),
        )
        outer = edges(*both(2 * blocks + odd_row), TL - 1, 0)
        inner = edges(*both(jnp.minimum(2 * i + 2, 2 * blocks - 1)), 0, 1)
        place(
            taps_ref,
            TL + 1,
            jnp.where(i == blocks - 1, below, next_ref[...]),
            jnp.where(i == blocks - 1, outer, inner),
        )
        for part in range(2):
            before, after = both(2 * i + part)
            merged = jnp.where(odd, after, pltpu.roll(before, 2, 1))
            for u in range(TL // 2):
                t = part * (TL // 2) + u
                cells = joined_ref[t * channels : (t + 1) * channels, :]
                place(taps_ref, t + 1, cells, pltpu.roll(merged, TL - 2 - 2 * u, 1))

    def convolve(taps_ref):
        pair = 2 * GROUP
        for i in range(TL // pair):
            base = i * pair * tap
            window = jnp.concatenate(
                [taps_ref[base + h * GROUP * tap : base + h * GROUP * tap + reach, :] for h in range(2)], axis=1
            )
            out = jnp.dot(weight_ref[...], window, preferred_element_type=jnp.float32)
            own = jnp.concatenate(
                [
                    jnp.concatenate(
                        [
                            taps_ref[base + (h * GROUP + r + 1) * tap + channels : base + (h * GROUP + r + 1) * tap + 2 * channels, :]
                            for r in range(GROUP)
                        ],
                        axis=0,
                    )
                    for h in range(2)
                ],
                axis=1,
            )
            out = out + jnp.dot(residual_ref[...], own, preferred_element_type=jnp.float32)
            out = out.reshape(channels, GROUP, 2 * TL)
            out = jnp.concatenate([out[:, :, :TL], out[:, :, TL:]], axis=1)
            texture_ref[:, i * pair : (i + 1) * pair, :] = out.astype(jnp.bfloat16)

    @pl.when(lax.rem(step, 2) == 0)
    def _():
        fill(even_ref)
        convolve(odd_ref)

    @pl.when(lax.rem(step, 2) == 1)
    def _():
        fill(odd_ref)
        convolve(even_ref)


def texture_call(place, joined, even_end, odd_end, even_rim, odd_rim, weight, residual):
    channels = even_end.shape[0]
    tiles = joined.shape[0] // channels
    blocks = tiles // TL
    def at(i):
        return jnp.minimum(i, blocks - 1)
    whole = lambda x: pl.BlockSpec(x.shape, lambda i: (0,) * x.ndim)
    return pl.pallas_call(
        texture_kernel,
        grid=(blocks + 1,),
        out_shape=jax.ShapeDtypeStruct((channels, tiles, TL), jnp.bfloat16),
        in_specs=[
            SCALARS,
            pl.BlockSpec((TL * channels, TL), lambda i: (at(i), 0)),
            pl.BlockSpec((channels, TL), lambda i: (jnp.maximum(at(i) * TL - 1, 0), 0)),
            pl.BlockSpec((channels, TL), lambda i: (jnp.minimum((at(i) + 1) * TL, tiles - 1), 0)),
        ] + [whole(x) for x in (even_end, odd_end, even_rim, odd_rim, weight, residual)],
        out_specs=pl.BlockSpec((channels, TL, TL), lambda i: (0, jnp.maximum(i - 1, 0), 0)),
        scratch_shapes=[pltpu.VMEM(((TL + 2) * 3 * channels, TL), jnp.bfloat16)] * 2,
        compiler_params=pltpu.CompilerParams(vmem_limit_bytes=VMEM_BYTES),
    )(place, joined, joined, joined, even_end, odd_end, even_rim, odd_rim, weight, residual)


def call(kernel, outs, scratch, specs):
    return pl.pallas_call(
        kernel,
        out_shape=outs,
        in_specs=specs,
        out_specs=jax.tree.map(lambda _: WHOLE, outs),
        scratch_shapes=scratch,
        compiler_params=pltpu.CompilerParams(vmem_limit_bytes=VMEM_BYTES),
    )


def local(
    image,
    conv_first,
    conv_second,
    conv_uv,
    send_block,
    send_shift,
    send_weight,
    send_count,
    recv_tile,
):
    half = jnp.bfloat16
    pixels = image[0]
    channels, strip_rows, width = pixels.shape
    by_row = pixels.transpose(1, 0, 2)
    place = jnp.stack(
        [lax.axis_index("row"), lax.axis_size("row"), lax.axis_index("cam")]
    ).astype(jnp.int32)
    odd = place[0] % 2 == 1
    near = swap(
        jnp.where(odd, by_row[:2], by_row[-2:]), jnp.where(odd, by_row[-2:], by_row[:2]), "row"
    )
    peers, capacity = send_block.shape[2:]
    entries = peers * capacity
    message = channels * capacity + capacity // 2
    used = lax.broadcasted_iota(jnp.int32, (peers, capacity), 1) < send_count.reshape(peers, 1)
    slots = (
        send_block[0, 0]
        + (send_shift[0, 0] << SHIFT_BIT)
        + (jnp.where(used, send_weight[0, 0], 0) << WEIGHT_BIT)
    )
    payload = call(
        send_kernel,
        jax.ShapeDtypeStruct((peers, message, TL), half),
        [
            pltpu.VMEM(((strip_rows + 4) * 3 * channels, width), half),
            pltpu.VMEM((strip_rows + 2, channels, width), half),
            pltpu.VMEM((strip_rows * width // TL, channels, TL), half),
            pltpu.VMEM((channels * capacity, TL), jnp.float32),
        ],
        [SCALARS] * 2 + [WHOLE] * 5,
    )(place, slots, by_row, *near, band(conv_first, False), band(conv_second, False))
    arrived = lax.all_to_all(payload, ("cam", "row"), split_axis=0, concat_axis=0, tiled=True)
    joined, edge, *ends = join_call(place, recv_tile.reshape(1, entries), arrived, channels)
    ends = swap(*ends, "row")
    rim = jnp.concatenate([edge, *ends], axis=1)
    rims = swap(rim, rim, "cam")
    same = (
        lax.broadcasted_iota(jnp.int32, (channels, GROUP, GROUP, channels), 0)
        == lax.broadcasted_iota(jnp.int32, (channels, GROUP, GROUP, channels), 3)
    ) & (
        lax.broadcasted_iota(jnp.int32, (channels, GROUP, GROUP, channels), 1)
        == lax.broadcasted_iota(jnp.int32, (channels, GROUP, GROUP, channels), 2)
    )
    residual = same.astype(half).reshape(channels * GROUP, GROUP * channels)
    return texture_call(place, joined, *ends, *rims, band(conv_uv, True), residual)


def solution(mesh):
    return jax.shard_map(
        local,
        mesh=mesh,
        in_specs=(
            P("cam", None, "row", None),
            P(),
            P(),
            P(),
            P("cam", "row", None, None),
            P("cam", "row", None, None),
            P("cam", "row", None, None),
            P("cam", "row", None),
            P("row", "cam", None, None),
        ),
        out_specs=P(None, "row", "cam"),
        check_vma=False,
    )
```

```python
import jax
import jax.numpy as jnp
from jax import lax
from jax.experimental import pallas as pl
from jax.experimental.pallas import tpu as pltpu
from jax.sharding import PartitionSpec as P

TL = 128
AR_DEV = 1024
GROUP = 8
CHUNK = 512
PAD = 4
SHIFT_BIT = 16
WEIGHT_BIT = 23
VMEM_BYTES = 32 * 1024 * 1024
SEND_BYTES = 36 * 1024 * 1024
WHOLE = pl.BlockSpec(memory_space=pltpu.VMEM)
SCALARS = pl.BlockSpec(memory_space=pltpu.SMEM)


def swap(even_pairs, odd_pairs, axis):
    count = lax.axis_size(axis)
    received = []
    for start, cells in enumerate((even_pairs, odd_pairs)):
        pairs = [(i, i + 1) for i in range(start, count - 1, 2)]
        received.append(lax.ppermute(cells, axis, pairs + [(j, i) for i, j in pairs]))
    return received


def ordered(odd, even_pairs, odd_pairs):
    return jnp.where(odd, even_pairs, odd_pairs), jnp.where(odd, odd_pairs, even_pairs)


def band(weight, channel_major):
    tap_row = weight.shape[1] // 3
    rows = [
        jnp.pad(weight, ((0, 0), (tap_row * r, tap_row * (GROUP - 1 - r)))) for r in range(GROUP)
    ]
    stacked = jnp.stack(rows, axis=1 if channel_major else 0)
    return stacked.reshape(-1, stacked.shape[-1])


def lanes_of(shape):
    return lax.broadcasted_iota(jnp.int32, shape, len(shape) - 1)


def send_kernel(
    place_ref,
    slot_ref,
    image_ref,
    even_ref,
    odd_ref,
    first_ref,
    second_ref,
    sent_ref,
    pixel_ref,
    taps_ref,
    hidden_ref,
    hidden_taps_ref,
    feature_ref,
    slots_ref,
    payload_ref,
    sent_sems,
):
    channels, rows, width = image_ref.shape
    tap = 3 * channels
    reach = (GROUP + 2) * tap
    lanes = lanes_of((channels, TL))
    zero = jnp.zeros((channels, TL), jnp.bfloat16)
    per_row = width // TL
    chunk = CHUNK // TL
    chunks = per_row // chunk
    odd = place_ref[0] % 2 == 1
    has_above = (place_ref[0] > 0).astype(jnp.float32)
    has_below = (place_ref[0] < place_ref[1] - 1).astype(jnp.float32)

    def spread(c, count, tile_of, out_ref):
        begin = c * chunk
        for i in range(count):
            tiles = [
                tile_of(i, m) if 0 <= m < per_row else zero
                for m in range(begin - 1, begin + chunk + 1)
            ]
            ahead = [pltpu.roll(cells, 1, 1) for cells in tiles[:-1]]
            back = [pltpu.roll(cells, TL - 1, 1) for cells in tiles[1:]]
            for k in range(chunk):
                cols = slice((begin + k) * TL, (begin + k + 1) * TL)
                base = i * tap
                out_ref[base : base + channels, cols] = jnp.where(lanes == 0, ahead[k], ahead[k + 1])
                out_ref[base + channels : base + 2 * channels, cols] = tiles[k + 1]
                out_ref[base + 2 * channels : base + tap, cols] = jnp.where(
                    lanes == TL - 1, back[k + 1], back[k]
                )

    def turn_rows(c):
        for m in range(c * chunk, (c + 1) * chunk):
            for q in range(channels):
                cells = image_ref[q, :, m * TL : (m + 1) * TL]
                base = q * (rows + PAD)
                pixel_ref[m, base : base + rows, :] = cells.astype(jnp.float32)

    def pixel_tile(i, m):
        cols = slice(m * TL, (m + 1) * TL)
        if i < 2 or i >= rows + 2:
            r = i if i < 2 else i - rows - 2
            above, below = ordered(odd, even_ref[r, :, cols], odd_ref[r, :, cols])
            return above if i < 2 else below
        return pixel_ref[m, pl.ds(i - 2, channels, stride=rows + PAD), :].astype(jnp.bfloat16)

    def hidden_tile(i, m):
        return hidden_ref[i, :, m * TL : (m + 1) * TL]

    def activate(v):
        half = 0.5 * v
        return half + half * jnp.tanh(half)

    step = 2 * TL

    def convolve_first(c):
        for j in range(c * CHUNK // step, (c + 1) * CHUNK // step):
            cols = slice(j * step, (j + 1) * step)
            for g in range(rows // GROUP):
                window = taps_ref[g * GROUP * tap : g * GROUP * tap + reach, cols]
                out = activate(jnp.dot(first_ref[...], window, preferred_element_type=jnp.float32))
                out = out.reshape(GROUP, channels, step)
                if g == 0:
                    out = jnp.concatenate([out[:1] * has_above, out[1:]], axis=0)
                hidden_ref[g * GROUP : (g + 1) * GROUP, :, cols] = out.astype(jnp.bfloat16)
            window = taps_ref[rows * tap : (rows + 4) * tap, cols]
            out = activate(
                jnp.dot(
                    first_ref[: 2 * channels, : 4 * tap], window, preferred_element_type=jnp.float32
                )
            ).reshape(2, channels, step)
            out = jnp.concatenate([out[:1], out[1:] * has_below], axis=0)
            hidden_ref[rows : rows + 2, :, cols] = out.astype(jnp.bfloat16)

    def convolve_second(c):
        for j in range(c * CHUNK // step, (c + 1) * CHUNK // step):
            cols = slice(j * step, (j + 1) * step)
            for g in range(rows // GROUP):
                window = hidden_taps_ref[g * GROUP * tap : g * GROUP * tap + reach, cols]
                out = jnp.dot(second_ref[...], window, preferred_element_type=jnp.float32)
                out = out.astype(jnp.bfloat16).reshape(GROUP, channels, step)
                for r in range(GROUP):
                    for half in range(2):
                        feature_ref[(g * GROUP + r) * per_row + 2 * j + half] = out[
                            r, :, half * TL : (half + 1) * TL
                        ]

    turn_rows(0)
    for s in range(chunks + 4):
        if s + 1 < chunks:
            turn_rows(s + 1)
        if s < chunks:
            spread(s, rows + 4, pixel_tile, taps_ref)
        if 0 <= s - 1 < chunks:
            convolve_first(s - 1)
        if 0 <= s - 3 < chunks:
            spread(s - 3, rows + 2, hidden_tile, hidden_taps_ref)
        if 0 <= s - 4 < chunks:
            convolve_second(s - 4)

    peers, capacity = slot_ref.shape
    half = capacity // 2
    side = lanes_of((half, TL)) < TL // 2
    slot_row = lax.broadcasted_iota(jnp.int32, (half, TL), 0)

    chunks = sent_sems.shape[0]
    batch = peers // chunks

    def flush(c):
        part = pl.ds(c * batch, batch)
        return pltpu.make_async_copy(payload_ref.at[part], sent_ref.at[part], sent_sems.at[c])

    @pl.loop(0, peers)
    def _(d):
        record = jnp.zeros((half, TL), jnp.float32)
        for k in range(capacity):
            slot = slot_ref[d, k]
            scale = lax.shift_right_logical(slot, WEIGHT_BIT).astype(jnp.float32) * 0.0625
            cells = feature_ref[slot & ((1 << SHIFT_BIT) - 1)]
            shift = lax.shift_right_logical(slot, SHIFT_BIT) & (TL - 1)
            cells = pltpu.roll(cells, shift, 1).astype(jnp.float32) * scale
            slots_ref[pl.ds(k, channels, stride=capacity + PAD), :] = cells
            here = (slot_row == k % half) & (side == (k < half))
            record = jnp.where(here, scale, record)
        for q in range(channels):
            base = q * (capacity + PAD)
            payload_ref[d, q * capacity : (q + 1) * capacity, :] = slots_ref[
                base : base + capacity, :
            ].astype(jnp.bfloat16)
        payload_ref[d, channels * capacity :, :] = record.astype(jnp.bfloat16)

        @pl.when(d % batch == batch - 1)
        def _():
            flush(d // batch).start()

    for c in range(chunks):
        flush(c).wait()


def scales_of(incoming_ref, entries):
    peers, message, lanes = incoming_ref.shape
    capacity = entries // peers
    half = capacity // 2
    record = incoming_ref[:, message - half :, :].astype(jnp.float32).reshape(peers * half, lanes)
    other = pltpu.roll(record, lanes // 2, 1)
    side = lanes_of(record.shape) < lanes // 2
    low = jnp.where(side, record, other).reshape(peers, half, lanes)
    high = jnp.where(side, other, record).reshape(peers, half, lanes)
    return jnp.concatenate([low, high], axis=1).reshape(entries, lanes).astype(jnp.bfloat16)


def join_kernel(
    place_ref,
    tile_ref,
    incoming_ref,
    joined_ref,
    edge_ref,
    even_ref,
    odd_ref,
    even_cells_ref,
    odd_cells_ref,
    scales_ref,
):
    peers = incoming_ref.shape[0]
    entries = tile_ref.shape[1]
    capacity = entries // peers
    channels = edge_ref.shape[0]
    blocks = joined_ref.shape[0] // (TL * channels)
    lanes = lanes_of((channels, TL))
    scales_ref[...] = scales_of(incoming_ref, entries)

    def gather(i, cells_ref):
        ids = lax.broadcasted_iota(jnp.int32, (TL, entries), 0) + i * TL
        onehot = jnp.where(ids == tile_ref[...], 1.0, 0.0).astype(jnp.bfloat16)
        total = jnp.dot(onehot, scales_ref[...], preferred_element_type=jnp.float32)
        inverse = 1.0 / jnp.maximum(total, 1.0)
        for q in range(0, channels, 2):
            pair = jnp.concatenate(
                [
                    incoming_ref[:, p * capacity : (p + 1) * capacity, :].reshape(entries, TL)
                    for p in (q, q + 1)
                ],
                axis=1,
            )
            total = jnp.dot(onehot, pair, preferred_element_type=jnp.float32)
            for p in range(2):
                cells_ref[pl.ds(q + p, TL, stride=channels + PAD), :] = (
                    total[:, p * TL : (p + 1) * TL] * inverse
                )

    def pack(i, cells_ref):
        for part in range(2):
            edge = jnp.zeros((channels, TL), jnp.bfloat16)
            for u in range(TL // 2):
                t = part * (TL // 2) + u
                base = t * (channels + PAD)
                cells = cells_ref[base : base + channels, :].astype(jnp.bfloat16)
                row = pl.multiple_of((i * TL + t) * channels, channels)
                joined_ref[pl.ds(row, channels), :] = cells
                edge = jnp.where(lanes // 2 == u, pltpu.roll(cells, 2 * u + 1, 1), edge)
            edge_ref[:, pl.ds(pl.multiple_of((2 * i + part) * TL, TL), TL)] = edge

    gather(0, even_cells_ref)

    @pl.loop(0, blocks // 2)
    def _(h):
        pack(2 * h, even_cells_ref)
        gather(2 * h + 1, odd_cells_ref)
        pack(2 * h + 1, odd_cells_ref)
        gather(jnp.minimum(2 * h + 2, blocks - 1), even_cells_ref)

    odd = place_ref[0] % 2 == 1
    head = joined_ref[:channels, :]
    tail = joined_ref[-channels:, :]
    even_ref[...] = jnp.where(odd, head, tail)
    odd_ref[...] = jnp.where(odd, tail, head)


def join_call(place, tiles, incoming, channels):
    half = jnp.bfloat16
    entries = tiles.shape[1]
    return pl.pallas_call(
        join_kernel,
        out_shape=(
            jax.ShapeDtypeStruct((AR_DEV * channels, TL), half),
            jax.ShapeDtypeStruct((channels, 2 * AR_DEV), half),
            jax.ShapeDtypeStruct((channels, TL), half),
            jax.ShapeDtypeStruct((channels, TL), half),
        ),
        in_specs=[SCALARS, WHOLE, WHOLE],
        out_specs=(WHOLE,) * 4,
        scratch_shapes=[
            pltpu.VMEM((TL * (channels + PAD), TL), jnp.float32),
            pltpu.VMEM((TL * (channels + PAD), TL), jnp.float32),
            pltpu.VMEM((entries, TL), half),
        ],
        compiler_params=pltpu.CompilerParams(vmem_limit_bytes=VMEM_BYTES),
    )(place, tiles, incoming)


def texture_kernel(
    place_ref,
    joined_ref,
    even_end_ref,
    odd_end_ref,
    even_rim_ref,
    odd_rim_ref,
    weight_ref,
    residual_ref,
    texture_ref,
    even_ref,
    odd_ref,
    even_out_ref,
    odd_out_ref,
    sems,
):
    channels = texture_ref.shape[0]
    blocks = texture_ref.shape[1] // TL
    tap = 3 * channels
    reach = (GROUP + 2) * tap
    lanes = lanes_of((channels, TL))
    odd_row = place_ref[0] % 2
    odd_cam = place_ref[2] % 2 == 1
    above, below = ordered(odd_row == 1, even_end_ref[...], odd_end_ref[...])

    def place(taps_ref, row, cells, edge):
        base = row * tap
        taps_ref[base : base + channels, :] = jnp.where(lanes == 0, edge, pltpu.roll(cells, 1, 1))
        taps_ref[base + channels : base + 2 * channels, :] = cells
        taps_ref[base + 2 * channels : base + 3 * channels, :] = jnp.where(
            lanes == TL - 1, edge, pltpu.roll(cells, TL - 1, 1)
        )

    def edges(before, after, before_lane, after_lane):
        return jnp.where(
            lanes == TL - 1,
            pltpu.roll(after, TL - 1 - after_lane, 1),
            pltpu.roll(before, TL - before_lane, 1),
        )

    def both(part):
        cols = pl.ds(pl.multiple_of(part * TL, TL), TL)
        return ordered(odd_cam, even_rim_ref[:, cols], odd_rim_ref[:, cols])

    def tile(t):
        return joined_ref[pl.ds(pl.multiple_of(t * channels, channels), channels), :]

    def fill(i, taps_ref):
        outer = edges(*both(2 * blocks + 1 - odd_row), TL - 1, 0)
        inner = edges(*both(jnp.maximum(2 * i - 1, 0)), TL - 2, TL - 1)
        cells = jnp.where(i == 0, above, tile(jnp.maximum(i * TL - 1, 0)))
        place(taps_ref, 0, cells, jnp.where(i == 0, outer, inner))
        last = blocks - 1
        outer = edges(*both(2 * blocks + odd_row), TL - 1, 0)
        inner = edges(*both(jnp.minimum(2 * i + 2, 2 * blocks - 1)), 0, 1)
        cells = jnp.where(i == last, below, tile(jnp.minimum((i + 1) * TL, blocks * TL - 1)))
        place(taps_ref, TL + 1, cells, jnp.where(i == last, outer, inner))
        for part in range(2):
            before, after = both(2 * i + part)
            merged = jnp.where(lanes % 2 == 1, after, pltpu.roll(before, 2, 1))
            for u in range(TL // 2):
                t = part * (TL // 2) + u
                place(taps_ref, t + 1, tile(i * TL + t), pltpu.roll(merged, TL - 2 - 2 * u, 1))

    def convolve(taps_ref, out_ref):
        pair = 2 * GROUP
        for i in range(TL // pair):
            base = i * pair * tap

            def side_by_side(start, size, rows):
                return jnp.concatenate(
                    [
                        jnp.concatenate(
                            [
                                taps_ref[at + k * tap : at + k * tap + size, :]
                                for k in range(rows)
                            ],
                            axis=0,
                        )
                        for at in (base + start, base + start + GROUP * tap)
                    ],
                    axis=1,
                )

            out = jnp.dot(
                weight_ref[...], side_by_side(0, reach, 1), preferred_element_type=jnp.float32
            )
            own = side_by_side(tap + channels, channels, GROUP)
            out = out + jnp.dot(residual_ref[...], own, preferred_element_type=jnp.float32)
            out = out.reshape(channels, GROUP, 2 * TL)
            out = jnp.concatenate([out[:, :, :TL], out[:, :, TL:]], axis=1)
            out_ref[:, i * pair : (i + 1) * pair, :] = out.astype(jnp.bfloat16)

    def flush(i, out_ref, slot):
        rows = pl.ds(pl.multiple_of(i * TL, TL), TL)
        return pltpu.make_async_copy(out_ref, texture_ref.at[:, rows, :], sems.at[slot])

    fill(0, even_ref)

    @pl.loop(0, blocks // 2)
    def _(h):
        @pl.when(h > 0)
        def _():
            flush(2 * h - 2, even_out_ref, 0).wait()

        fill(2 * h + 1, odd_ref)
        convolve(even_ref, even_out_ref)
        flush(2 * h, even_out_ref, 0).start()

        @pl.when(h > 0)
        def _():
            flush(2 * h - 1, odd_out_ref, 1).wait()

        fill(jnp.minimum(2 * h + 2, blocks - 1), even_ref)
        convolve(odd_ref, odd_out_ref)
        flush(2 * h + 1, odd_out_ref, 1).start()

    flush(blocks - 2, even_out_ref, 0).wait()
    flush(blocks - 1, odd_out_ref, 1).wait()


def texture_call(place, joined, even_end, odd_end, even_rim, odd_rim, weight, residual):
    channels = even_end.shape[0]
    half = jnp.bfloat16
    taps = pltpu.VMEM(((TL + 2) * 3 * channels, TL), half)
    block = pltpu.VMEM((channels, TL, TL), half)
    return pl.pallas_call(
        texture_kernel,
        out_shape=jax.ShapeDtypeStruct((channels, joined.shape[0] // channels, TL), half),
        in_specs=[SCALARS] + [WHOLE] * 7,
        out_specs=pl.BlockSpec(memory_space=pl.ANY),
        scratch_shapes=[taps, taps, block, block, pltpu.SemaphoreType.DMA((2,))],
        compiler_params=pltpu.CompilerParams(vmem_limit_bytes=VMEM_BYTES),
    )(place, joined, even_end, odd_end, even_rim, odd_rim, weight, residual)


def local(
    image,
    conv_first,
    conv_second,
    conv_uv,
    send_block,
    send_shift,
    send_weight,
    send_count,
    recv_tile,
):
    half = jnp.bfloat16
    pixels = image[0]
    channels, strip_rows, width = pixels.shape
    place = jnp.stack(
        [lax.axis_index("row"), lax.axis_size("row"), lax.axis_index("cam")]
    ).astype(jnp.int32)
    odd = place[0] % 2 == 1
    head = pixels[:, :2].transpose(1, 0, 2)
    tail = pixels[:, -2:].transpose(1, 0, 2)
    near = swap(jnp.where(odd, head, tail), jnp.where(odd, tail, head), "row")
    peers, capacity = send_block.shape[2:]
    entries = peers * capacity
    message = channels * capacity + capacity // 2
    used = lax.broadcasted_iota(jnp.int32, (peers, capacity), 1) < send_count.reshape(peers, 1)
    slots = (
        send_block[0, 0]
        + (send_shift[0, 0] << SHIFT_BIT)
        + (jnp.where(used, send_weight[0, 0], 0) << WEIGHT_BIT)
    )
    payload = pl.pallas_call(
        send_kernel,
        out_shape=jax.ShapeDtypeStruct((peers, message, TL), half),
        scratch_shapes=[
            pltpu.VMEM((width // TL, channels * (strip_rows + PAD), TL), jnp.float32),
            pltpu.VMEM(((strip_rows + 4) * 3 * channels, width), half),
            pltpu.VMEM((strip_rows + 2, channels, width), half),
            pltpu.VMEM(((strip_rows + 2) * 3 * channels, width), half),
            pltpu.VMEM((strip_rows * width // TL, channels, TL), half),
            pltpu.VMEM((channels * (capacity + PAD), TL), jnp.float32),
            pltpu.VMEM((peers, message, TL), half),
            pltpu.SemaphoreType.DMA((8,)),
        ],
        in_specs=[SCALARS] * 2 + [WHOLE] * 5,
        out_specs=pl.BlockSpec(memory_space=pl.ANY),
        compiler_params=pltpu.CompilerParams(vmem_limit_bytes=SEND_BYTES),
    )(place, slots, pixels, *near, band(conv_first, False), band(conv_second, False))
    arrived = lax.all_to_all(payload, ("cam", "row"), split_axis=0, concat_axis=0, tiled=True)
    joined, edge, *ends = join_call(place, recv_tile.reshape(1, entries), arrived, channels)
    ends = swap(*ends, "row")
    rim = jnp.concatenate([edge, *ends], axis=1)
    rims = swap(rim, rim, "cam")
    same = (
        lax.broadcasted_iota(jnp.int32, (channels, GROUP, GROUP, channels), 0)
        == lax.broadcasted_iota(jnp.int32, (channels, GROUP, GROUP, channels), 3)
    ) & (
        lax.broadcasted_iota(jnp.int32, (channels, GROUP, GROUP, channels), 1)
        == lax.broadcasted_iota(jnp.int32, (channels, GROUP, GROUP, channels), 2)
    )
    residual = same.astype(half).reshape(channels * GROUP, GROUP * channels)
    return texture_call(place, joined, *ends, *rims, band(conv_uv, True), residual)


def solution(mesh):
    return jax.shard_map(
        local,
        mesh=mesh,
        in_specs=(
            P("cam", None, "row", None),
            P(),
            P(),
            P(),
            P("cam", "row", None, None),
            P("cam", "row", None, None),
            P("cam", "row", None, None),
            P("cam", "row", None),
            P("row", "cam", None, None),
        ),
        out_specs=P(None, "row", "cam"),
        check_vma=False,
    )
```

```python
import jax
import jax.numpy as jnp
from jax import lax
from jax.experimental import pallas as pl
from jax.experimental.pallas import tpu as pltpu
from jax.sharding import PartitionSpec as P

TL = 128
AR_DEV = 1024
GROUP = 8
CHUNK = 512
PAD = 4
SHIFT_BIT = 16
WEIGHT_BIT = 23
VMEM_BYTES = 32 * 1024 * 1024
SEND_BYTES = 36 * 1024 * 1024
WHOLE = pl.BlockSpec(memory_space=pltpu.VMEM)
SCALARS = pl.BlockSpec(memory_space=pltpu.SMEM)


def swap(even_pairs, odd_pairs, axis):
    count = lax.axis_size(axis)
    received = []
    for start, cells in enumerate((even_pairs, odd_pairs)):
        pairs = [(i, i + 1) for i in range(start, count - 1, 2)]
        received.append(lax.ppermute(cells, axis, pairs + [(j, i) for i, j in pairs]))
    return received


def ordered(odd, even_pairs, odd_pairs):
    return jnp.where(odd, even_pairs, odd_pairs), jnp.where(odd, odd_pairs, even_pairs)


def band(weight, channel_major):
    tap_row = weight.shape[1] // 3
    rows = [
        jnp.pad(weight, ((0, 0), (tap_row * r, tap_row * (GROUP - 1 - r)))) for r in range(GROUP)
    ]
    stacked = jnp.stack(rows, axis=1 if channel_major else 0)
    return stacked.reshape(-1, stacked.shape[-1])


def lanes_of(shape):
    return lax.broadcasted_iota(jnp.int32, shape, len(shape) - 1)


def send_kernel(
    place_ref,
    slot_ref,
    image_ref,
    even_ref,
    odd_ref,
    first_kernel_ref,
    second_kernel_ref,
    sent_ref,
    first_ref,
    second_ref,
    pixel_ref,
    taps_ref,
    hidden_ref,
    hidden_taps_ref,
    feature_ref,
    payload_ref,
    sent_sems,
    *slots_refs,
):
    channels, rows, width = image_ref.shape
    tap = 3 * channels
    reach = (GROUP + 2) * tap
    lanes = lanes_of((channels, TL))
    zero = jnp.zeros((channels, TL), jnp.bfloat16)
    per_row = width // TL
    chunk = CHUNK // TL
    chunks = per_row // chunk
    odd = place_ref[0] % 2 == 1
    has_above = (place_ref[0] > 0).astype(jnp.float32)
    has_below = (place_ref[0] < place_ref[1] - 1).astype(jnp.float32)

    def spread(c, count, tile_of, out_ref):
        begin = c * chunk
        for i in range(count):
            tiles = [
                tile_of(i, m) if 0 <= m < per_row else zero
                for m in range(begin - 1, begin + chunk + 1)
            ]
            ahead = [pltpu.roll(cells, 1, 1) for cells in tiles[:-1]]
            back = [pltpu.roll(cells, TL - 1, 1) for cells in tiles[1:]]
            for k in range(chunk):
                cols = slice((begin + k) * TL, (begin + k + 1) * TL)
                base = i * tap
                out_ref[base : base + channels, cols] = jnp.where(lanes == 0, ahead[k], ahead[k + 1])
                out_ref[base + channels : base + 2 * channels, cols] = tiles[k + 1]
                out_ref[base + 2 * channels : base + tap, cols] = jnp.where(
                    lanes == TL - 1, back[k + 1], back[k]
                )

    def turn_rows(c):
        for m in range(c * chunk, (c + 1) * chunk):
            for q in range(channels):
                cells = image_ref[q, :, m * TL : (m + 1) * TL]
                base = q * (rows + PAD)
                pixel_ref[m, base : base + rows, :] = cells.astype(jnp.float32)

    def pixel_tile(i, m):
        cols = slice(m * TL, (m + 1) * TL)
        if i < 2 or i >= rows + 2:
            r = i if i < 2 else i - rows - 2
            above, below = ordered(odd, even_ref[r, :, cols], odd_ref[r, :, cols])
            return above if i < 2 else below
        return pixel_ref[m, pl.ds(i - 2, channels, stride=rows + PAD), :].astype(jnp.bfloat16)

    def hidden_tile(i, m):
        return hidden_ref[i, :, m * TL : (m + 1) * TL]

    for kernel_ref, band_ref in ((first_kernel_ref, first_ref), (second_kernel_ref, second_ref)):
        band_ref[...] = jnp.zeros_like(band_ref)
        for r in range(GROUP):
            reached = slice(r * tap, (r + 3) * tap)
            band_ref[r * channels : (r + 1) * channels, reached] = kernel_ref[...]

    def activate(v):
        half = 0.5 * v
        return half + half * jnp.tanh(half)

    step = 2 * TL

    def convolve_first(c):
        for j in range(c * CHUNK // step, (c + 1) * CHUNK // step):
            cols = slice(j * step, (j + 1) * step)
            for g in range(rows // GROUP):
                window = taps_ref[g * GROUP * tap : g * GROUP * tap + reach, cols]
                out = activate(jnp.dot(first_ref[...], window, preferred_element_type=jnp.float32))
                out = out.reshape(GROUP, channels, step)
                if g == 0:
                    out = jnp.concatenate([out[:1] * has_above, out[1:]], axis=0)
                hidden_ref[g * GROUP : (g + 1) * GROUP, :, cols] = out.astype(jnp.bfloat16)
            window = taps_ref[rows * tap : (rows + 4) * tap, cols]
            out = activate(
                jnp.dot(
                    first_ref[: 2 * channels, : 4 * tap], window, preferred_element_type=jnp.float32
                )
            ).reshape(2, channels, step)
            out = jnp.concatenate([out[:1], out[1:] * has_below], axis=0)
            hidden_ref[rows : rows + 2, :, cols] = out.astype(jnp.bfloat16)

    def convolve_second(c):
        for j in range(c * CHUNK // step, (c + 1) * CHUNK // step):
            cols = slice(j * step, (j + 1) * step)
            for g in range(rows // GROUP):
                window = hidden_taps_ref[g * GROUP * tap : g * GROUP * tap + reach, cols]
                out = jnp.dot(second_ref[...], window, preferred_element_type=jnp.float32)
                out = out.astype(jnp.bfloat16).reshape(GROUP, channels, step)
                for r in range(GROUP):
                    for half in range(2):
                        feature_ref[(g * GROUP + r) * per_row + 2 * j + half] = out[
                            r, :, half * TL : (half + 1) * TL
                        ]

    turn_rows(0)
    for s in range(chunks + 4):
        if s + 1 < chunks:
            turn_rows(s + 1)
        if s < chunks:
            spread(s, rows + 4, pixel_tile, taps_ref)
        if 0 <= s - 1 < chunks:
            convolve_first(s - 1)
        if 0 <= s - 3 < chunks:
            spread(s - 3, rows + 2, hidden_tile, hidden_taps_ref)
        if 0 <= s - 4 < chunks:
            convolve_second(s - 4)

    peers, capacity = slot_ref.shape
    half = capacity // 2
    side = lanes_of((half, TL)) < TL // 2
    slot_row = lax.broadcasted_iota(jnp.int32, (half, TL), 0)

    chunks = sent_sems.shape[0]
    batch = peers // chunks

    def flush(c):
        part = pl.ds(c * batch, batch)
        return pltpu.make_async_copy(payload_ref.at[part], sent_ref.at[part], sent_sems.at[c])

    def send_to(d, slots_ref):
        record = jnp.zeros((half, TL), jnp.float32)
        for k in range(capacity):
            slot = slot_ref[d, k]
            scale = lax.shift_right_logical(slot, WEIGHT_BIT).astype(jnp.float32) * 0.0625
            cells = feature_ref[slot & ((1 << SHIFT_BIT) - 1)]
            shift = lax.shift_right_logical(slot, SHIFT_BIT) & (TL - 1)
            cells = pltpu.roll(cells, shift, 1).astype(jnp.float32) * scale
            slots_ref[pl.ds(k, channels, stride=capacity + PAD), :] = cells
            here = (slot_row == k % half) & (side == (k < half))
            record = jnp.where(here, scale, record)
        for q in range(channels):
            base = q * (capacity + PAD)
            payload_ref[d, q * capacity : (q + 1) * capacity, :] = slots_ref[
                base : base + capacity, :
            ].astype(jnp.bfloat16)
        payload_ref[d, channels * capacity :, :] = record.astype(jnp.bfloat16)

    @pl.loop(0, chunks)
    def _(c):
        for u in range(batch):
            send_to(c * batch + u, slots_refs[u % len(slots_refs)])
        flush(c).start()

    for c in range(chunks):
        flush(c).wait()


def scales_of(incoming_ref, entries):
    peers, message, lanes = incoming_ref.shape
    capacity = entries // peers
    half = capacity // 2
    record = incoming_ref[:, message - half :, :].astype(jnp.float32).reshape(peers * half, lanes)
    other = pltpu.roll(record, lanes // 2, 1)
    side = lanes_of(record.shape) < lanes // 2
    low = jnp.where(side, record, other).reshape(peers, half, lanes)
    high = jnp.where(side, other, record).reshape(peers, half, lanes)
    return jnp.concatenate([low, high], axis=1).reshape(entries, lanes).astype(jnp.bfloat16)


def join_kernel(
    place_ref,
    tile_ref,
    incoming_ref,
    joined_ref,
    plain_ref,
    edge_ref,
    even_ref,
    odd_ref,
    even_cells_ref,
    odd_cells_ref,
    scales_ref,
):
    peers = incoming_ref.shape[0]
    entries = tile_ref.shape[1]
    capacity = entries // peers
    channels = edge_ref.shape[0]
    blocks = joined_ref.shape[0] // (TL * channels)
    lanes = lanes_of((channels, TL))
    scales_ref[...] = scales_of(incoming_ref, entries)

    def gather(i, cells_ref):
        ids = lax.broadcasted_iota(jnp.int32, (TL, entries), 0) + i * TL
        onehot = jnp.where(ids == tile_ref[...], 1.0, 0.0).astype(jnp.bfloat16)
        total = jnp.dot(onehot, scales_ref[...], preferred_element_type=jnp.float32)
        inverse = 1.0 / jnp.maximum(total, 1.0)
        for q in range(0, channels, 2):
            pair = jnp.concatenate(
                [
                    incoming_ref[:, p * capacity : (p + 1) * capacity, :].reshape(entries, TL)
                    for p in (q, q + 1)
                ],
                axis=1,
            )
            total = jnp.dot(onehot, pair, preferred_element_type=jnp.float32)
            for p in range(2):
                cells = total[:, p * TL : (p + 1) * TL] * inverse
                cells_ref[pl.ds(q + p, TL, stride=channels + PAD), :] = cells
                rows = pl.ds(pl.multiple_of(i * TL, TL), TL)
                plain_ref[q + p, rows, :] = cells.astype(jnp.bfloat16)

    def pack(i, cells_ref):
        for part in range(2):
            edge = jnp.zeros((channels, TL), jnp.bfloat16)
            for u in range(TL // 2):
                t = part * (TL // 2) + u
                base = t * (channels + PAD)
                cells = cells_ref[base : base + channels, :].astype(jnp.bfloat16)
                row = pl.multiple_of((i * TL + t) * channels, channels)
                joined_ref[pl.ds(row, channels), :] = cells
                edge = jnp.where(lanes // 2 == u, pltpu.roll(cells, 2 * u + 1, 1), edge)
            edge_ref[:, pl.ds(pl.multiple_of((2 * i + part) * TL, TL), TL)] = edge

    gather(0, even_cells_ref)

    @pl.loop(0, blocks // 2)
    def _(h):
        pack(2 * h, even_cells_ref)
        gather(2 * h + 1, odd_cells_ref)
        pack(2 * h + 1, odd_cells_ref)
        gather(jnp.minimum(2 * h + 2, blocks - 1), even_cells_ref)

    odd = place_ref[0] % 2 == 1
    head = joined_ref[:channels, :]
    tail = joined_ref[-channels:, :]
    even_ref[...] = jnp.where(odd, head, tail)
    odd_ref[...] = jnp.where(odd, tail, head)


def join_call(place, tiles, incoming, channels):
    half = jnp.bfloat16
    entries = tiles.shape[1]
    return pl.pallas_call(
        join_kernel,
        out_shape=(
            jax.ShapeDtypeStruct((AR_DEV * channels, TL), half),
            jax.ShapeDtypeStruct((channels, AR_DEV, TL), half),
            jax.ShapeDtypeStruct((channels, 2 * AR_DEV), half),
            jax.ShapeDtypeStruct((channels, TL), half),
            jax.ShapeDtypeStruct((channels, TL), half),
        ),
        in_specs=[SCALARS, WHOLE, WHOLE],
        out_specs=(WHOLE,) * 5,
        scratch_shapes=[
            pltpu.VMEM((TL * (channels + PAD), TL), jnp.float32),
            pltpu.VMEM((TL * (channels + PAD), TL), jnp.float32),
            pltpu.VMEM((entries, TL), half),
        ],
        compiler_params=pltpu.CompilerParams(vmem_limit_bytes=VMEM_BYTES),
    )(place, tiles, incoming)


def texture_kernel(
    place_ref,
    joined_ref,
    plain_ref,
    even_end_ref,
    odd_end_ref,
    even_rim_ref,
    odd_rim_ref,
    weight_ref,
    texture_ref,
    even_ref,
    odd_ref,
    even_out_ref,
    odd_out_ref,
    sems,
):
    channels = texture_ref.shape[0]
    blocks = texture_ref.shape[1] // TL
    tap = 3 * channels
    reach = (GROUP + 2) * tap
    lanes = lanes_of((channels, TL))
    odd_row = place_ref[0] % 2
    odd_cam = place_ref[2] % 2 == 1
    above, below = ordered(odd_row == 1, even_end_ref[...], odd_end_ref[...])

    def place(taps_ref, row, cells, edge):
        base = row * tap
        taps_ref[base : base + channels, :] = jnp.where(lanes == 0, edge, pltpu.roll(cells, 1, 1))
        taps_ref[base + channels : base + 2 * channels, :] = cells
        taps_ref[base + 2 * channels : base + 3 * channels, :] = jnp.where(
            lanes == TL - 1, edge, pltpu.roll(cells, TL - 1, 1)
        )

    def edges(before, after, before_lane, after_lane):
        return jnp.where(
            lanes == TL - 1,
            pltpu.roll(after, TL - 1 - after_lane, 1),
            pltpu.roll(before, TL - before_lane, 1),
        )

    def both(part):
        cols = pl.ds(pl.multiple_of(part * TL, TL), TL)
        return ordered(odd_cam, even_rim_ref[:, cols], odd_rim_ref[:, cols])

    def tile(t):
        return joined_ref[pl.ds(pl.multiple_of(t * channels, channels), channels), :]

    def fill(i, taps_ref):
        outer = edges(*both(2 * blocks + 1 - odd_row), TL - 1, 0)
        inner = edges(*both(jnp.maximum(2 * i - 1, 0)), TL - 2, TL - 1)
        cells = jnp.where(i == 0, above, tile(jnp.maximum(i * TL - 1, 0)))
        place(taps_ref, 0, cells, jnp.where(i == 0, outer, inner))
        last = blocks - 1
        outer = edges(*both(2 * blocks + odd_row), TL - 1, 0)
        inner = edges(*both(jnp.minimum(2 * i + 2, 2 * blocks - 1)), 0, 1)
        cells = jnp.where(i == last, below, tile(jnp.minimum((i + 1) * TL, blocks * TL - 1)))
        place(taps_ref, TL + 1, cells, jnp.where(i == last, outer, inner))
        for part in range(2):
            before, after = both(2 * i + part)
            merged = jnp.where(lanes % 2 == 1, after, pltpu.roll(before, 2, 1))
            for u in range(TL // 2):
                t = part * (TL // 2) + u
                place(taps_ref, t + 1, tile(i * TL + t), pltpu.roll(merged, TL - 2 - 2 * u, 1))

    def convolve(i, taps_ref, out_ref):
        pair = 2 * GROUP
        for k in range(TL // pair):
            base = k * pair * tap
            window = jnp.concatenate(
                [taps_ref[at : at + reach, :] for at in (base, base + GROUP * tap)], axis=1
            )
            out = jnp.dot(weight_ref[...], window, preferred_element_type=jnp.float32)
            out = out.reshape(channels, GROUP, 2 * TL)
            out = jnp.concatenate([out[:, :, :TL], out[:, :, TL:]], axis=1)
            rows = pl.ds(pl.multiple_of(i * TL + k * pair, pair), pair)
            out = out + plain_ref[:, rows, :].astype(jnp.float32)
            out_ref[:, k * pair : (k + 1) * pair, :] = out.astype(jnp.bfloat16)

    def flush(i, out_ref, slot):
        rows = pl.ds(pl.multiple_of(i * TL, TL), TL)
        return pltpu.make_async_copy(out_ref, texture_ref.at[:, rows, :], sems.at[slot])

    fill(0, even_ref)

    @pl.loop(0, blocks // 2)
    def _(h):
        @pl.when(h > 0)
        def _():
            flush(2 * h - 2, even_out_ref, 0).wait()

        fill(2 * h + 1, odd_ref)
        convolve(2 * h, even_ref, even_out_ref)
        flush(2 * h, even_out_ref, 0).start()

        @pl.when(h > 0)
        def _():
            flush(2 * h - 1, odd_out_ref, 1).wait()

        fill(jnp.minimum(2 * h + 2, blocks - 1), even_ref)
        convolve(2 * h + 1, odd_ref, odd_out_ref)
        flush(2 * h + 1, odd_out_ref, 1).start()

    flush(blocks - 2, even_out_ref, 0).wait()
    flush(blocks - 1, odd_out_ref, 1).wait()


def texture_call(place, joined, plain, *edges):
    channels = plain.shape[0]
    half = jnp.bfloat16
    taps = pltpu.VMEM(((TL + 2) * 3 * channels, TL), half)
    block = pltpu.VMEM((channels, TL, TL), half)
    return pl.pallas_call(
        texture_kernel,
        out_shape=jax.ShapeDtypeStruct(plain.shape, half),
        in_specs=[SCALARS] + [WHOLE] * (2 + len(edges)),
        out_specs=pl.BlockSpec(memory_space=pl.ANY),
        scratch_shapes=[taps, taps, block, block, pltpu.SemaphoreType.DMA((2,))],
        compiler_params=pltpu.CompilerParams(vmem_limit_bytes=VMEM_BYTES),
    )(place, joined, plain, *edges)


def local(
    image,
    conv_first,
    conv_second,
    conv_uv,
    send_block,
    send_shift,
    send_weight,
    send_count,
    recv_tile,
):
    half = jnp.bfloat16
    pixels = image[0]
    channels, strip_rows, width = pixels.shape
    place = jnp.stack(
        [lax.axis_index("row"), lax.axis_size("row"), lax.axis_index("cam")]
    ).astype(jnp.int32)
    odd = place[0] % 2 == 1
    head = pixels[:, :2].transpose(1, 0, 2)
    tail = pixels[:, -2:].transpose(1, 0, 2)
    near = swap(jnp.where(odd, head, tail), jnp.where(odd, tail, head), "row")
    peers, capacity = send_block.shape[2:]
    entries = peers * capacity
    message = channels * capacity + capacity // 2
    used = lax.broadcasted_iota(jnp.int32, (peers, capacity), 1) < send_count.reshape(peers, 1)
    slots = (
        send_block[0, 0]
        + (send_shift[0, 0] << SHIFT_BIT)
        + (jnp.where(used, send_weight[0, 0], 0) << WEIGHT_BIT)
    )
    payload = pl.pallas_call(
        send_kernel,
        out_shape=jax.ShapeDtypeStruct((peers, message, TL), half),
        scratch_shapes=[
            pltpu.VMEM((GROUP * channels, (GROUP + 2) * 3 * channels), half),
            pltpu.VMEM((GROUP * channels, (GROUP + 2) * 3 * channels), half),
            pltpu.VMEM((width // TL, channels * (strip_rows + PAD), TL), jnp.float32),
            pltpu.VMEM(((strip_rows + 4) * 3 * channels, width), half),
            pltpu.VMEM((strip_rows + 2, channels, width), half),
            pltpu.VMEM(((strip_rows + 2) * 3 * channels, width), half),
            pltpu.VMEM((strip_rows * width // TL, channels, TL), half),
            pltpu.VMEM((peers, message, TL), half),
            pltpu.SemaphoreType.DMA((8,)),
        ]
        + [pltpu.VMEM((channels * (capacity + PAD), TL), jnp.float32) for _ in range(4)],
        in_specs=[SCALARS] * 2 + [WHOLE] * 5,
        out_specs=pl.BlockSpec(memory_space=pl.ANY),
        compiler_params=pltpu.CompilerParams(vmem_limit_bytes=SEND_BYTES),
    )(place, slots, pixels, *near, conv_first, conv_second)
    arrived = lax.all_to_all(payload, ("cam", "row"), split_axis=0, concat_axis=0, tiled=True)
    joined, plain, edge, *ends = join_call(place, recv_tile.reshape(1, entries), arrived, channels)
    ends = swap(*ends, "row")
    rim = jnp.concatenate([edge, *ends], axis=1)
    rims = swap(rim, rim, "cam")
    return texture_call(place, joined, plain, *ends, *rims, band(conv_uv, True))


def solution(mesh):
    return jax.shard_map(
        local,
        mesh=mesh,
        in_specs=(
            P("cam", None, "row", None),
            P(),
            P(),
            P(),
            P("cam", "row", None, None),
            P("cam", "row", None, None),
            P("cam", "row", None, None),
            P("cam", "row", None),
            P("row", "cam", None, None),
        ),
        out_specs=P(None, "row", "cam"),
        check_vma=False,
    )
```

```python
import jax
import jax.numpy as jnp
from jax import lax
from jax.experimental import pallas as pl
from jax.experimental.pallas import tpu as pltpu
from jax.sharding import PartitionSpec as P

TL = 128
AR_DEV = 1024
GROUP = 8
CHUNK = 512
PAD = 4
SHIFT_BIT = 16
WEIGHT_BIT = 23
VMEM_BYTES = 32 * 1024 * 1024
SEND_BYTES = 24 * 1024 * 1024
STRIP_BYTES = 12 * 1024 * 1024
WHOLE = pl.BlockSpec(memory_space=pltpu.VMEM)
SCALARS = pl.BlockSpec(memory_space=pltpu.SMEM)


def swap(even_pairs, odd_pairs, axis):
    count = lax.axis_size(axis)
    received = []
    for start, cells in enumerate((even_pairs, odd_pairs)):
        pairs = [(i, i + 1) for i in range(start, count - 1, 2)]
        received.append(lax.ppermute(cells, axis, pairs + [(j, i) for i, j in pairs]))
    return received


def ordered(odd, even_pairs, odd_pairs):
    return jnp.where(odd, even_pairs, odd_pairs), jnp.where(odd, odd_pairs, even_pairs)


def band(weight, channel_major):
    tap_row = weight.shape[1] // 3
    rows = [
        jnp.pad(weight, ((0, 0), (tap_row * r, tap_row * (GROUP - 1 - r)))) for r in range(GROUP)
    ]
    stacked = jnp.stack(rows, axis=1 if channel_major else 0)
    return stacked.reshape(-1, stacked.shape[-1])


def lanes_of(shape):
    return lax.broadcasted_iota(jnp.int32, shape, len(shape) - 1)


def spread(lanes, begin, count, per_row, base_of, tiles_of, out_ref):
    channels = lanes.shape[0]
    zero = jnp.zeros((channels, TL), jnp.bfloat16)
    for base, tile_of in zip(base_of, tiles_of):
        tiles = [
            tile_of(m) if 0 <= m < per_row else zero for m in range(begin - 1, begin + count + 1)
        ]
        ahead = [pltpu.roll(cells, 1, 1) for cells in tiles[:-1]]
        back = [pltpu.roll(cells, TL - 1, 1) for cells in tiles[1:]]
        for k in range(count):
            cols = slice((begin + k) * TL, (begin + k + 1) * TL)
            out_ref[base : base + channels, cols] = jnp.where(lanes == 0, ahead[k], ahead[k + 1])
            out_ref[base + channels : base + 2 * channels, cols] = tiles[k + 1]
            out_ref[base + 2 * channels : base + 3 * channels, cols] = jnp.where(
                lanes == TL - 1, back[k + 1], back[k]
            )


def strip_kernel(image_ref, taps_ref, pixel_ref):
    channels, rows, width = image_ref.shape
    lanes = lanes_of((channels, TL))
    per_row = width // TL
    chunk = CHUNK // TL

    def turn_rows(c):
        for m in range(c * chunk, (c + 1) * chunk):
            for q in range(channels):
                cells = image_ref[q, :, m * TL : (m + 1) * TL]
                base = q * (rows + PAD)
                pixel_ref[m, base : base + rows, :] = cells.astype(jnp.float32)

    def tile_of(i):
        return lambda m: pixel_ref[m, pl.ds(i, channels, stride=rows + PAD), :].astype(jnp.bfloat16)

    turn_rows(0)
    for c in range(per_row // chunk):
        if (c + 1) * chunk < per_row:
            turn_rows(c + 1)
        spread(
            lanes,
            c * chunk,
            chunk,
            per_row,
            [i * 3 * channels for i in range(rows)],
            [tile_of(i) for i in range(rows)],
            taps_ref,
        )


def send_kernel(
    place_ref,
    slot_ref,
    strip_ref,
    even_ref,
    odd_ref,
    first_kernel_ref,
    second_kernel_ref,
    sent_ref,
    halo_ref,
    first_ref,
    second_ref,
    hidden_ref,
    hidden_taps_ref,
    feature_ref,
    payload_ref,
    sent_sems,
    *slots_refs,
):
    channels = even_ref.shape[1]
    width = even_ref.shape[2]
    tap = 3 * channels
    rows = strip_ref.shape[0] // tap
    reach = (GROUP + 2) * tap
    lanes = lanes_of((channels, TL))
    per_row = width // TL
    chunk = CHUNK // TL
    chunks = per_row // chunk
    odd = place_ref[0] % 2 == 1
    has_above = (place_ref[0] > 0).astype(jnp.float32)
    has_below = (place_ref[0] < place_ref[1] - 1).astype(jnp.float32)

    def halo_tile(r, side):
        def tile_of(m):
            cols = slice(m * TL, (m + 1) * TL)
            return ordered(odd, even_ref[r, :, cols], odd_ref[r, :, cols])[side]

        return tile_of

    def hidden_tile(i):
        return lambda m: hidden_ref[i, :, m * TL : (m + 1) * TL]

    halo = [(r, side) for side in range(2) for r in range(2)]

    def spread_halo(c):
        spread(
            lanes,
            c * chunk,
            chunk,
            per_row,
            [i * tap for i in range(len(halo))],
            [halo_tile(*at) for at in halo],
            halo_ref,
        )

    def spread_hidden(c):
        spread(
            lanes,
            c * chunk,
            chunk,
            per_row,
            [i * tap for i in range(rows + 2)],
            [hidden_tile(i) for i in range(rows + 2)],
            hidden_taps_ref,
        )

    for kernel_ref, band_ref in ((first_kernel_ref, first_ref), (second_kernel_ref, second_ref)):
        band_ref[...] = jnp.zeros_like(band_ref)
        for r in range(GROUP):
            reached = slice(r * tap, (r + 3) * tap)
            band_ref[r * channels : (r + 1) * channels, reached] = kernel_ref[...]

    def activate(v):
        half = 0.5 * v
        return half + half * jnp.tanh(half)

    step = 2 * TL

    def convolve_first(c):
        for j in range(c * CHUNK // step, (c + 1) * CHUNK // step):
            cols = slice(j * step, (j + 1) * step)
            for g in range(rows // GROUP):
                begin = (g * GROUP - 2) * tap
                if g == 0:
                    window = jnp.concatenate(
                        [halo_ref[: 2 * tap, cols], strip_ref[: begin + reach, cols]], axis=0
                    )
                else:
                    window = strip_ref[begin : begin + reach, cols]
                out = activate(jnp.dot(first_ref[...], window, preferred_element_type=jnp.float32))
                out = out.reshape(GROUP, channels, step)
                if g == 0:
                    out = jnp.concatenate([out[:1] * has_above, out[1:]], axis=0)
                hidden_ref[g * GROUP : (g + 1) * GROUP, :, cols] = out.astype(jnp.bfloat16)
            window = jnp.concatenate(
                [strip_ref[(rows - 2) * tap :, cols], halo_ref[2 * tap :, cols]], axis=0
            )
            out = activate(
                jnp.dot(
                    first_ref[: 2 * channels, : 4 * tap], window, preferred_element_type=jnp.float32
                )
            ).reshape(2, channels, step)
            out = jnp.concatenate([out[:1], out[1:] * has_below], axis=0)
            hidden_ref[rows : rows + 2, :, cols] = out.astype(jnp.bfloat16)

    def convolve_second(c):
        for j in range(c * CHUNK // step, (c + 1) * CHUNK // step):
            cols = slice(j * step, (j + 1) * step)
            for g in range(rows // GROUP):
                window = hidden_taps_ref[g * GROUP * tap : g * GROUP * tap + reach, cols]
                out = jnp.dot(second_ref[...], window, preferred_element_type=jnp.float32)
                out = out.astype(jnp.bfloat16).reshape(GROUP, channels, step)
                for r in range(GROUP):
                    for half in range(2):
                        feature_ref[(g * GROUP + r) * per_row + 2 * j + half] = out[
                            r, :, half * TL : (half + 1) * TL
                        ]

    for s in range(chunks + 3):
        if s < chunks:
            spread_halo(s)
            convolve_first(s)
        if 0 <= s - 2 < chunks:
            spread_hidden(s - 2)
        if 0 <= s - 3 < chunks:
            convolve_second(s - 3)

    peers, capacity = slot_ref.shape
    half = capacity // 2
    side = lanes_of((half, TL)) < TL // 2
    slot_row = lax.broadcasted_iota(jnp.int32, (half, TL), 0)

    chunks = sent_sems.shape[0]
    batch = peers // chunks

    def flush(c):
        part = pl.ds(c * batch, batch)
        return pltpu.make_async_copy(payload_ref.at[part], sent_ref.at[part], sent_sems.at[c])

    def send_to(d, slots_ref):
        record = jnp.zeros((half, TL), jnp.float32)
        for k in range(capacity):
            slot = slot_ref[d, k]
            scale = lax.shift_right_logical(slot, WEIGHT_BIT).astype(jnp.float32) * 0.0625
            cells = feature_ref[slot & ((1 << SHIFT_BIT) - 1)]
            shift = lax.shift_right_logical(slot, SHIFT_BIT) & (TL - 1)
            cells = pltpu.roll(cells, shift, 1).astype(jnp.float32) * scale
            slots_ref[pl.ds(k, channels, stride=capacity + PAD), :] = cells
            here = (slot_row == k % half) & (side == (k < half))
            record = jnp.where(here, scale, record)
        for q in range(channels):
            base = q * (capacity + PAD)
            payload_ref[d, q * capacity : (q + 1) * capacity, :] = slots_ref[
                base : base + capacity, :
            ].astype(jnp.bfloat16)
        payload_ref[d, channels * capacity :, :] = record.astype(jnp.bfloat16)

    @pl.loop(0, chunks)
    def _(c):
        for u in range(batch):
            send_to(c * batch + u, slots_refs[u % len(slots_refs)])
        flush(c).start()

    for c in range(chunks):
        flush(c).wait()


def scales_of(incoming_ref, entries):
    peers, message, lanes = incoming_ref.shape
    capacity = entries // peers
    half = capacity // 2
    record = incoming_ref[:, message - half :, :].astype(jnp.float32).reshape(peers * half, lanes)
    other = pltpu.roll(record, lanes // 2, 1)
    side = lanes_of(record.shape) < lanes // 2
    low = jnp.where(side, record, other).reshape(peers, half, lanes)
    high = jnp.where(side, other, record).reshape(peers, half, lanes)
    return jnp.concatenate([low, high], axis=1).reshape(entries, lanes).astype(jnp.bfloat16)


def join_kernel(
    place_ref,
    tile_ref,
    incoming_ref,
    joined_ref,
    plain_ref,
    edge_ref,
    even_ref,
    odd_ref,
    even_cells_ref,
    odd_cells_ref,
    scales_ref,
):
    peers = incoming_ref.shape[0]
    entries = tile_ref.shape[1]
    capacity = entries // peers
    channels = edge_ref.shape[0]
    blocks = joined_ref.shape[0] // (TL * channels)
    lanes = lanes_of((channels, TL))
    scales_ref[...] = scales_of(incoming_ref, entries)

    def gather(i, cells_ref):
        ids = lax.broadcasted_iota(jnp.int32, (TL, entries), 0) + i * TL
        onehot = jnp.where(ids == tile_ref[...], 1.0, 0.0).astype(jnp.bfloat16)
        total = jnp.dot(onehot, scales_ref[...], preferred_element_type=jnp.float32)
        inverse = 1.0 / jnp.maximum(total, 1.0)
        for q in range(0, channels, 2):
            pair = jnp.concatenate(
                [
                    incoming_ref[:, p * capacity : (p + 1) * capacity, :].reshape(entries, TL)
                    for p in (q, q + 1)
                ],
                axis=1,
            )
            total = jnp.dot(onehot, pair, preferred_element_type=jnp.float32)
            for p in range(2):
                cells = total[:, p * TL : (p + 1) * TL] * inverse
                cells_ref[pl.ds(q + p, TL, stride=channels + PAD), :] = cells
                rows = pl.ds(pl.multiple_of(i * TL, TL), TL)
                plain_ref[q + p, rows, :] = cells.astype(jnp.bfloat16)

    def pack(i, cells_ref):
        for part in range(2):
            edge = jnp.zeros((channels, TL), jnp.bfloat16)
            for u in range(TL // 2):
                t = part * (TL // 2) + u
                base = t * (channels + PAD)
                cells = cells_ref[base : base + channels, :].astype(jnp.bfloat16)
                row = pl.multiple_of((i * TL + t) * channels, channels)
                joined_ref[pl.ds(row, channels), :] = cells
                edge = jnp.where(lanes // 2 == u, pltpu.roll(cells, 2 * u + 1, 1), edge)
            edge_ref[:, pl.ds(pl.multiple_of((2 * i + part) * TL, TL), TL)] = edge

    gather(0, even_cells_ref)

    @pl.loop(0, blocks // 2)
    def _(h):
        pack(2 * h, even_cells_ref)
        gather(2 * h + 1, odd_cells_ref)
        pack(2 * h + 1, odd_cells_ref)
        gather(jnp.minimum(2 * h + 2, blocks - 1), even_cells_ref)

    odd = place_ref[0] % 2 == 1
    head = joined_ref[:channels, :]
    tail = joined_ref[-channels:, :]
    even_ref[...] = jnp.where(odd, head, tail)
    odd_ref[...] = jnp.where(odd, tail, head)


def join_call(place, tiles, incoming, channels):
    half = jnp.bfloat16
    entries = tiles.shape[1]
    return pl.pallas_call(
        join_kernel,
        out_shape=(
            jax.ShapeDtypeStruct((AR_DEV * channels, TL), half),
            jax.ShapeDtypeStruct((channels, AR_DEV, TL), half),
            jax.ShapeDtypeStruct((channels, 2 * AR_DEV), half),
            jax.ShapeDtypeStruct((channels, TL), half),
            jax.ShapeDtypeStruct((channels, TL), half),
        ),
        in_specs=[SCALARS, WHOLE, WHOLE],
        out_specs=(WHOLE,) * 5,
        scratch_shapes=[
            pltpu.VMEM((TL * (channels + PAD), TL), jnp.float32),
            pltpu.VMEM((TL * (channels + PAD), TL), jnp.float32),
            pltpu.VMEM((entries, TL), half),
        ],
        compiler_params=pltpu.CompilerParams(vmem_limit_bytes=VMEM_BYTES),
    )(place, tiles, incoming)


def texture_kernel(
    place_ref,
    joined_ref,
    plain_ref,
    even_end_ref,
    odd_end_ref,
    even_rim_ref,
    odd_rim_ref,
    weight_ref,
    texture_ref,
    even_ref,
    odd_ref,
    even_out_ref,
    odd_out_ref,
    sems,
):
    channels = texture_ref.shape[0]
    blocks = texture_ref.shape[1] // TL
    tap = 3 * channels
    reach = (GROUP + 2) * tap
    lanes = lanes_of((channels, TL))
    odd_row = place_ref[0] % 2
    odd_cam = place_ref[2] % 2 == 1
    above, below = ordered(odd_row == 1, even_end_ref[...], odd_end_ref[...])

    def place(taps_ref, row, cells, edge):
        base = row * tap
        taps_ref[base : base + channels, :] = jnp.where(lanes == 0, edge, pltpu.roll(cells, 1, 1))
        taps_ref[base + channels : base + 2 * channels, :] = cells
        taps_ref[base + 2 * channels : base + 3 * channels, :] = jnp.where(
            lanes == TL - 1, edge, pltpu.roll(cells, TL - 1, 1)
        )

    def edges(before, after, before_lane, after_lane):
        return jnp.where(
            lanes == TL - 1,
            pltpu.roll(after, TL - 1 - after_lane, 1),
            pltpu.roll(before, TL - before_lane, 1),
        )

    def both(part):
        cols = pl.ds(pl.multiple_of(part * TL, TL), TL)
        return ordered(odd_cam, even_rim_ref[:, cols], odd_rim_ref[:, cols])

    def tile(t):
        return joined_ref[pl.ds(pl.multiple_of(t * channels, channels), channels), :]

    def fill(i, taps_ref):
        outer = edges(*both(2 * blocks + 1 - odd_row), TL - 1, 0)
        inner = edges(*both(jnp.maximum(2 * i - 1, 0)), TL - 2, TL - 1)
        cells = jnp.where(i == 0, above, tile(jnp.maximum(i * TL - 1, 0)))
        place(taps_ref, 0, cells, jnp.where(i == 0, outer, inner))
        last = blocks - 1
        outer = edges(*both(2 * blocks + odd_row), TL - 1, 0)
        inner = edges(*both(jnp.minimum(2 * i + 2, 2 * blocks - 1)), 0, 1)
        cells = jnp.where(i == last, below, tile(jnp.minimum((i + 1) * TL, blocks * TL - 1)))
        place(taps_ref, TL + 1, cells, jnp.where(i == last, outer, inner))
        for part in range(2):
            before, after = both(2 * i + part)
            merged = jnp.where(lanes % 2 == 1, after, pltpu.roll(before, 2, 1))
            for u in range(TL // 2):
                t = part * (TL // 2) + u
                place(taps_ref, t + 1, tile(i * TL + t), pltpu.roll(merged, TL - 2 - 2 * u, 1))

    def convolve(i, taps_ref, out_ref):
        pair = 2 * GROUP
        for k in range(TL // pair):
            base = k * pair * tap
            window = jnp.concatenate(
                [taps_ref[at : at + reach, :] for at in (base, base + GROUP * tap)], axis=1
            )
            out = jnp.dot(weight_ref[...], window, preferred_element_type=jnp.float32)
            out = out.reshape(channels, GROUP, 2 * TL)
            out = jnp.concatenate([out[:, :, :TL], out[:, :, TL:]], axis=1)
            rows = pl.ds(pl.multiple_of(i * TL + k * pair, pair), pair)
            out = out + plain_ref[:, rows, :].astype(jnp.float32)
            out_ref[:, k * pair : (k + 1) * pair, :] = out.astype(jnp.bfloat16)

    def flush(i, out_ref, slot):
        rows = pl.ds(pl.multiple_of(i * TL, TL), TL)
        return pltpu.make_async_copy(out_ref, texture_ref.at[:, rows, :], sems.at[slot])

    fill(0, even_ref)

    @pl.loop(0, blocks // 2)
    def _(h):
        @pl.when(h > 0)
        def _():
            flush(2 * h - 2, even_out_ref, 0).wait()

        fill(2 * h + 1, odd_ref)
        convolve(2 * h, even_ref, even_out_ref)
        flush(2 * h, even_out_ref, 0).start()

        @pl.when(h > 0)
        def _():
            flush(2 * h - 1, odd_out_ref, 1).wait()

        fill(jnp.minimum(2 * h + 2, blocks - 1), even_ref)
        convolve(2 * h + 1, odd_ref, odd_out_ref)
        flush(2 * h + 1, odd_out_ref, 1).start()

    flush(blocks - 2, even_out_ref, 0).wait()
    flush(blocks - 1, odd_out_ref, 1).wait()


def texture_call(place, joined, plain, *edges):
    channels = plain.shape[0]
    half = jnp.bfloat16
    taps = pltpu.VMEM(((TL + 2) * 3 * channels, TL), half)
    block = pltpu.VMEM((channels, TL, TL), half)
    return pl.pallas_call(
        texture_kernel,
        out_shape=jax.ShapeDtypeStruct(plain.shape, half),
        in_specs=[SCALARS] + [WHOLE] * (2 + len(edges)),
        out_specs=pl.BlockSpec(memory_space=pl.ANY),
        scratch_shapes=[taps, taps, block, block, pltpu.SemaphoreType.DMA((2,))],
        compiler_params=pltpu.CompilerParams(vmem_limit_bytes=VMEM_BYTES),
    )(place, joined, plain, *edges)


def local(
    image,
    conv_first,
    conv_second,
    conv_uv,
    send_block,
    send_shift,
    send_weight,
    send_count,
    recv_tile,
):
    half = jnp.bfloat16
    pixels = image[0]
    channels, strip_rows, width = pixels.shape
    place = jnp.stack(
        [lax.axis_index("row"), lax.axis_size("row"), lax.axis_index("cam")]
    ).astype(jnp.int32)
    odd = place[0] % 2 == 1
    head = pixels[:, :2].transpose(1, 0, 2)
    tail = pixels[:, -2:].transpose(1, 0, 2)
    near = swap(jnp.where(odd, head, tail), jnp.where(odd, tail, head), "row")
    peers, capacity = send_block.shape[2:]
    entries = peers * capacity
    message = channels * capacity + capacity // 2
    used = lax.broadcasted_iota(jnp.int32, (peers, capacity), 1) < send_count.reshape(peers, 1)
    slots = (
        send_block[0, 0]
        + (send_shift[0, 0] << SHIFT_BIT)
        + (jnp.where(used, send_weight[0, 0], 0) << WEIGHT_BIT)
    )
    taps = jax.ShapeDtypeStruct((strip_rows * 3 * channels, width), half)
    strip = pl.pallas_call(
        strip_kernel,
        out_shape=taps,
        in_specs=[WHOLE],
        out_specs=WHOLE,
        scratch_shapes=[
            pltpu.VMEM((width // TL, channels * (strip_rows + PAD), TL), jnp.float32)
        ],
        compiler_params=pltpu.CompilerParams(vmem_limit_bytes=STRIP_BYTES),
        cost_estimate=pl.CostEstimate(flops=0, bytes_accessed=taps.size * 2, transcendentals=0),
    )(pixels)
    bands = pltpu.VMEM((GROUP * channels, (GROUP + 2) * 3 * channels), half)
    payload = pl.pallas_call(
        send_kernel,
        out_shape=jax.ShapeDtypeStruct((peers, message, TL), half),
        scratch_shapes=[
            pltpu.VMEM((4 * 3 * channels, width), half),
            bands,
            bands,
            pltpu.VMEM((strip_rows + 2, channels, width), half),
            pltpu.VMEM(((strip_rows + 2) * 3 * channels, width), half),
            pltpu.VMEM((strip_rows * width // TL, channels, TL), half),
            pltpu.VMEM((peers, message, TL), half),
            pltpu.SemaphoreType.DMA((8,)),
        ]
        + [pltpu.VMEM((channels * (capacity + PAD), TL), jnp.float32) for _ in range(4)],
        in_specs=[SCALARS] * 2 + [WHOLE] * 5,
        out_specs=pl.BlockSpec(memory_space=pl.ANY),
        compiler_params=pltpu.CompilerParams(vmem_limit_bytes=SEND_BYTES),
    )(place, slots, strip, *near, conv_first, conv_second)
    arrived = lax.all_to_all(payload, ("cam", "row"), split_axis=0, concat_axis=0, tiled=True)
    joined, plain, edge, *ends = join_call(place, recv_tile.reshape(1, entries), arrived, channels)
    ends = swap(*ends, "row")
    rim = jnp.concatenate([edge, *ends], axis=1)
    rims = swap(rim, rim, "cam")
    return texture_call(place, joined, plain, *ends, *rims, band(conv_uv, True))


def solution(mesh):
    return jax.shard_map(
        local,
        mesh=mesh,
        in_specs=(
            P("cam", None, "row", None),
            P(),
            P(),
            P(),
            P("cam", "row", None, None),
            P("cam", "row", None, None),
            P("cam", "row", None, None),
            P("cam", "row", None),
            P("row", "cam", None, None),
        ),
        out_specs=P(None, "row", "cam"),
        check_vma=False,
    )
```

```python
import jax
import jax.numpy as jnp
from jax import lax
from jax.experimental import pallas as pl
from jax.experimental.pallas import tpu as pltpu
from jax.sharding import PartitionSpec as P


TL = 128
AR_DEV = 1024
GROUP = 8
CHUNK = 512
PAD = 4
SHIFT_BIT = 16
WEIGHT_BIT = 23
VMEM_BYTES = 32 * 1024 * 1024
SEND_BYTES = 20 * 1024 * 1024
STRIP_BYTES = 24 * 1024 * 1024
WHOLE = pl.BlockSpec(memory_space=pltpu.VMEM)
SCALARS = pl.BlockSpec(memory_space=pltpu.SMEM)


def swap(even_pairs, odd_pairs, axis):
    count = lax.axis_size(axis)
    received = []
    for start, cells in enumerate((even_pairs, odd_pairs)):
        pairs = [(i, i + 1) for i in range(start, count - 1, 2)]
        received.append(lax.ppermute(cells, axis, pairs + [(j, i) for i, j in pairs]))
    return received


def ordered(odd, even_pairs, odd_pairs):
    return jnp.where(odd, even_pairs, odd_pairs), jnp.where(odd, odd_pairs, even_pairs)


def band(weight, channel_major):
    tap_row = weight.shape[1] // 3
    rows = [
        jnp.pad(weight, ((0, 0), (tap_row * r, tap_row * (GROUP - 1 - r)))) for r in range(GROUP)
    ]
    stacked = jnp.stack(rows, axis=1 if channel_major else 0)
    return stacked.reshape(-1, stacked.shape[-1])


def lanes_of(shape):
    return lax.broadcasted_iota(jnp.int32, shape, len(shape) - 1)


def spread(lanes, begin, count, per_row, base_of, tiles_of, out_ref):
    channels = lanes.shape[0]
    zero = jnp.zeros((channels, TL), jnp.bfloat16)
    for base, tile_of in zip(base_of, tiles_of):
        tiles = [
            tile_of(m) if 0 <= m < per_row else zero for m in range(begin - 1, begin + count + 1)
        ]
        ahead = [pltpu.roll(cells, 1, 1) for cells in tiles[:-1]]
        back = [pltpu.roll(cells, TL - 1, 1) for cells in tiles[1:]]
        for k in range(count):
            cols = slice((begin + k) * TL, (begin + k + 1) * TL)
            out_ref[base : base + channels, cols] = jnp.where(lanes == 0, ahead[k], ahead[k + 1])
            out_ref[base + channels : base + 2 * channels, cols] = tiles[k + 1]
            out_ref[base + 2 * channels : base + 3 * channels, cols] = jnp.where(
                lanes == TL - 1, back[k + 1], back[k]
            )


def build_band(kernel_ref, band_ref):
    channels, tap = kernel_ref.shape[0], kernel_ref.shape[1] // 3
    band_ref[...] = jnp.zeros_like(band_ref)
    for r in range(GROUP):
        reached = slice(r * tap, (r + 3) * tap)
        band_ref[r * channels : (r + 1) * channels, reached] = kernel_ref[...]


def activate(v):
    half = 0.5 * v
    return half + half * jnp.tanh(half)


def strip_kernel(image_ref, kernel_ref, taps_ref, hidden_taps_ref, pixel_ref, hidden_ref, band_ref):
    channels, rows, width = image_ref.shape
    tap = 3 * channels
    reach = (GROUP + 2) * tap
    lanes = lanes_of((channels, TL))
    per_row = width // TL
    chunk = CHUNK // TL
    chunks = per_row // chunk
    inner = rows - GROUP
    step = 2 * TL
    build_band(kernel_ref, band_ref)

    def turn_rows(c):
        for m in range(c * chunk, (c + 1) * chunk):
            for q in range(channels):
                cells = image_ref[q, :, m * TL : (m + 1) * TL]
                base = q * (rows + PAD)
                pixel_ref[m, base : base + rows, :] = cells.astype(jnp.float32)

    def tile_of(i):
        return lambda m: pixel_ref[m, pl.ds(i, channels, stride=rows + PAD), :].astype(jnp.bfloat16)

    def hidden_tile(i):
        return lambda m: hidden_ref[i, :, m * TL : (m + 1) * TL]

    def spread_rows(c, count, tile_at, out_ref):
        spread(
            lanes,
            c * chunk,
            chunk,
            per_row,
            [i * tap for i in range(count)],
            [tile_at(i) for i in range(count)],
            out_ref,
        )

    def convolve(c):
        for j in range(c * CHUNK // step, (c + 1) * CHUNK // step):
            cols = slice(j * step, (j + 1) * step)
            for g in range(inner // GROUP):
                begin = ((g + 1) * GROUP - 2) * tap
                window = taps_ref[begin : begin + reach, cols]
                out = activate(jnp.dot(band_ref[...], window, preferred_element_type=jnp.float32))
                out = out.reshape(GROUP, channels, step).astype(jnp.bfloat16)
                hidden_ref[g * GROUP : (g + 1) * GROUP, :, cols] = out

    turn_rows(0)
    for s in range(chunks + 3):
        if s + 1 < chunks:
            turn_rows(s + 1)
        if s < chunks:
            spread_rows(s, rows, tile_of, taps_ref)
        if 0 <= s - 1 < chunks:
            convolve(s - 1)
        if 0 <= s - 3 < chunks:
            spread_rows(s - 3, inner, hidden_tile, hidden_taps_ref)


def send_kernel(
    place_ref,
    slot_ref,
    strip_ref,
    inner_ref,
    even_ref,
    odd_ref,
    first_kernel_ref,
    second_kernel_ref,
    sent_ref,
    halo_ref,
    first_ref,
    second_ref,
    hidden_ref,
    outer_ref,
    feature_ref,
    payload_ref,
    sent_sems,
    *slots_refs,
):
    channels = even_ref.shape[1]
    width = even_ref.shape[2]
    tap = 3 * channels
    rows = strip_ref.shape[0] // tap
    reach = (GROUP + 2) * tap
    lanes = lanes_of((channels, TL))
    per_row = width // TL
    chunk = CHUNK // TL
    chunks = per_row // chunk
    step = 2 * TL
    odd = place_ref[0] % 2 == 1
    has_above = (place_ref[0] > 0).astype(jnp.float32)
    has_below = (place_ref[0] < place_ref[1] - 1).astype(jnp.float32)
    build_band(first_kernel_ref, first_ref)
    build_band(second_kernel_ref, second_ref)

    def halo_tile(side, r):
        def tile_of(m):
            cols = slice(m * TL, (m + 1) * TL)
            return ordered(odd, even_ref[r, :, cols], odd_ref[r, :, cols])[side]

        return tile_of

    def hidden_tile(i):
        return lambda m: hidden_ref[i, :, m * TL : (m + 1) * TL]

    def spread_rows(c, tiles_of, out_ref):
        bases = [i * tap for i in range(len(tiles_of))]
        spread(lanes, c * chunk, chunk, per_row, bases, tiles_of, out_ref)

    halo = [halo_tile(side, r) for side in range(2) for r in range(2)]
    outer = [hidden_tile(i) for i in range(GROUP + 2)]

    def convolve_first(c):
        for j in range(c * CHUNK // step, (c + 1) * CHUNK // step):
            cols = slice(j * step, (j + 1) * step)
            window = jnp.concatenate(
                [halo_ref[: 2 * tap, cols], strip_ref[: GROUP * tap, cols]], axis=0
            )
            out = activate(jnp.dot(first_ref[...], window, preferred_element_type=jnp.float32))
            out = out.reshape(GROUP, channels, step)
            out = jnp.concatenate([out[:1] * has_above, out[1:]], axis=0)
            hidden_ref[:GROUP, :, cols] = out.astype(jnp.bfloat16)
            window = jnp.concatenate(
                [strip_ref[(rows - 2) * tap :, cols], halo_ref[2 * tap :, cols]], axis=0
            )
            out = activate(
                jnp.dot(
                    first_ref[: 2 * channels, : 4 * tap], window, preferred_element_type=jnp.float32
                )
            ).reshape(2, channels, step)
            out = jnp.concatenate([out[:1], out[1:] * has_below], axis=0)
            hidden_ref[GROUP:, :, cols] = out.astype(jnp.bfloat16)

    def convolve_second(c):
        for j in range(c * CHUNK // step, (c + 1) * CHUNK // step):
            cols = slice(j * step, (j + 1) * step)
            for g in range(rows // GROUP):
                begin = (g - 1) * GROUP * tap
                if g == 0:
                    window = jnp.concatenate(
                        [outer_ref[: GROUP * tap, cols], inner_ref[: 2 * tap, cols]], axis=0
                    )
                elif g == rows // GROUP - 1:
                    window = jnp.concatenate(
                        [inner_ref[begin:, cols], outer_ref[GROUP * tap :, cols]], axis=0
                    )
                else:
                    window = inner_ref[begin : begin + reach, cols]
                out = jnp.dot(second_ref[...], window, preferred_element_type=jnp.float32)
                out = out.astype(jnp.bfloat16).reshape(GROUP, channels, step)
                for r in range(GROUP):
                    for half in range(2):
                        feature_ref[(g * GROUP + r) * per_row + 2 * j + half] = out[
                            r, :, half * TL : (half + 1) * TL
                        ]

    for s in range(chunks + 3):
        if s < chunks:
            spread_rows(s, halo, halo_ref)
            convolve_first(s)
        if 0 <= s - 2 < chunks:
            spread_rows(s - 2, outer, outer_ref)
        if 0 <= s - 3 < chunks:
            convolve_second(s - 3)

    peers, capacity = slot_ref.shape
    half = capacity // 2
    side = lanes_of((half, TL)) < TL // 2
    slot_row = lax.broadcasted_iota(jnp.int32, (half, TL), 0)

    chunks = sent_sems.shape[0]
    batch = peers // chunks

    def flush(c):
        part = pl.ds(c * batch, batch)
        return pltpu.make_async_copy(payload_ref.at[part], sent_ref.at[part], sent_sems.at[c])

    def send_to(d, slots_ref):
        record = jnp.zeros((half, TL), jnp.float32)
        for k in range(capacity):
            slot = slot_ref[d, k]
            scale = lax.shift_right_logical(slot, WEIGHT_BIT).astype(jnp.float32) * 0.0625
            cells = feature_ref[slot & ((1 << SHIFT_BIT) - 1)]
            shift = lax.shift_right_logical(slot, SHIFT_BIT) & (TL - 1)
            cells = pltpu.roll(cells, shift, 1).astype(jnp.float32) * scale
            slots_ref[pl.ds(k, channels, stride=capacity + PAD), :] = cells
            here = (slot_row == k % half) & (side == (k < half))
            record = jnp.where(here, scale, record)
        for q in range(channels):
            base = q * (capacity + PAD)
            payload_ref[d, q * capacity : (q + 1) * capacity, :] = slots_ref[
                base : base + capacity, :
            ].astype(jnp.bfloat16)
        payload_ref[d, channels * capacity :, :] = record.astype(jnp.bfloat16)

    @pl.loop(0, chunks)
    def _(c):
        for u in range(batch):
            send_to(c * batch + u, slots_refs[u % len(slots_refs)])
        flush(c).start()

    for c in range(chunks):
        flush(c).wait()


def scales_of(incoming_ref, entries):
    peers, message, lanes = incoming_ref.shape
    capacity = entries // peers
    half = capacity // 2
    record = incoming_ref[:, message - half :, :].astype(jnp.float32).reshape(peers * half, lanes)
    other = pltpu.roll(record, lanes // 2, 1)
    side = lanes_of(record.shape) < lanes // 2
    low = jnp.where(side, record, other).reshape(peers, half, lanes)
    high = jnp.where(side, other, record).reshape(peers, half, lanes)
    return jnp.concatenate([low, high], axis=1).reshape(entries, lanes).astype(jnp.bfloat16)


def join_kernel(
    place_ref,
    tile_ref,
    incoming_ref,
    joined_ref,
    plain_ref,
    edge_ref,
    even_ref,
    odd_ref,
    even_cells_ref,
    odd_cells_ref,
    scales_ref,
):
    peers = incoming_ref.shape[0]
    entries = tile_ref.shape[1]
    capacity = entries // peers
    channels = edge_ref.shape[0]
    blocks = joined_ref.shape[0] // (TL * channels)
    lanes = lanes_of((channels, TL))
    scales_ref[...] = scales_of(incoming_ref, entries)

    def gather(i, cells_ref):
        ids = lax.broadcasted_iota(jnp.int32, (TL, entries), 0) + i * TL
        onehot = jnp.where(ids == tile_ref[...], 1.0, 0.0).astype(jnp.bfloat16)
        total = jnp.dot(onehot, scales_ref[...], preferred_element_type=jnp.float32)
        inverse = 1.0 / jnp.maximum(total, 1.0)
        for q in range(0, channels, 2):
            pair = jnp.concatenate(
                [
                    incoming_ref[:, p * capacity : (p + 1) * capacity, :].reshape(entries, TL)
                    for p in (q, q + 1)
                ],
                axis=1,
            )
            total = jnp.dot(onehot, pair, preferred_element_type=jnp.float32)
            for p in range(2):
                cells = total[:, p * TL : (p + 1) * TL] * inverse
                cells_ref[pl.ds(q + p, TL, stride=channels + PAD), :] = cells
                rows = pl.ds(pl.multiple_of(i * TL, TL), TL)
                plain_ref[q + p, rows, :] = cells.astype(jnp.bfloat16)

    def pack(i, cells_ref):
        for part in range(2):
            edge = jnp.zeros((channels, TL), jnp.bfloat16)
            for u in range(TL // 2):
                t = part * (TL // 2) + u
                base = t * (channels + PAD)
                cells = cells_ref[base : base + channels, :].astype(jnp.bfloat16)
                row = pl.multiple_of((i * TL + t) * channels, channels)
                joined_ref[pl.ds(row, channels), :] = cells
                edge = jnp.where(lanes // 2 == u, pltpu.roll(cells, 2 * u + 1, 1), edge)
            edge_ref[:, pl.ds(pl.multiple_of((2 * i + part) * TL, TL), TL)] = edge

    gather(0, even_cells_ref)

    @pl.loop(0, blocks // 2)
    def _(h):
        pack(2 * h, even_cells_ref)
        gather(2 * h + 1, odd_cells_ref)
        pack(2 * h + 1, odd_cells_ref)
        gather(jnp.minimum(2 * h + 2, blocks - 1), even_cells_ref)

    odd = place_ref[0] % 2 == 1
    head = joined_ref[:channels, :]
    tail = joined_ref[-channels:, :]
    even_ref[...] = jnp.where(odd, head, tail)
    odd_ref[...] = jnp.where(odd, tail, head)


def join_call(place, tiles, incoming, channels):
    half = jnp.bfloat16
    entries = tiles.shape[1]
    return pl.pallas_call(
        join_kernel,
        out_shape=(
            jax.ShapeDtypeStruct((AR_DEV * channels, TL), half),
            jax.ShapeDtypeStruct((channels, AR_DEV, TL), half),
            jax.ShapeDtypeStruct((channels, 2 * AR_DEV), half),
            jax.ShapeDtypeStruct((channels, TL), half),
            jax.ShapeDtypeStruct((channels, TL), half),
        ),
        in_specs=[SCALARS, WHOLE, WHOLE],
        out_specs=(WHOLE,) * 5,
        scratch_shapes=[
            pltpu.VMEM((TL * (channels + PAD), TL), jnp.float32),
            pltpu.VMEM((TL * (channels + PAD), TL), jnp.float32),
            pltpu.VMEM((entries, TL), half),
        ],
        compiler_params=pltpu.CompilerParams(vmem_limit_bytes=VMEM_BYTES),
    )(place, tiles, incoming)


def texture_kernel(
    place_ref,
    joined_ref,
    plain_ref,
    even_end_ref,
    odd_end_ref,
    even_rim_ref,
    odd_rim_ref,
    weight_ref,
    texture_ref,
    even_ref,
    odd_ref,
    even_out_ref,
    odd_out_ref,
    sems,
):
    channels = texture_ref.shape[0]
    blocks = texture_ref.shape[1] // TL
    tap = 3 * channels
    reach = (GROUP + 2) * tap
    lanes = lanes_of((channels, TL))
    odd_row = place_ref[0] % 2
    odd_cam = place_ref[2] % 2 == 1
    above, below = ordered(odd_row == 1, even_end_ref[...], odd_end_ref[...])

    def place(taps_ref, row, cells, edge):
        base = row * tap
        taps_ref[base : base + channels, :] = jnp.where(lanes == 0, edge, pltpu.roll(cells, 1, 1))
        taps_ref[base + channels : base + 2 * channels, :] = cells
        taps_ref[base + 2 * channels : base + 3 * channels, :] = jnp.where(
            lanes == TL - 1, edge, pltpu.roll(cells, TL - 1, 1)
        )

    def edges(before, after, before_lane, after_lane):
        return jnp.where(
            lanes == TL - 1,
            pltpu.roll(after, TL - 1 - after_lane, 1),
            pltpu.roll(before, TL - before_lane, 1),
        )

    def both(part):
        cols = pl.ds(pl.multiple_of(part * TL, TL), TL)
        return ordered(odd_cam, even_rim_ref[:, cols], odd_rim_ref[:, cols])

    def tile(t):
        return joined_ref[pl.ds(pl.multiple_of(t * channels, channels), channels), :]

    def fill(i, taps_ref):
        outer = edges(*both(2 * blocks + 1 - odd_row), TL - 1, 0)
        inner = edges(*both(jnp.maximum(2 * i - 1, 0)), TL - 2, TL - 1)
        cells = jnp.where(i == 0, above, tile(jnp.maximum(i * TL - 1, 0)))
        place(taps_ref, 0, cells, jnp.where(i == 0, outer, inner))
        last = blocks - 1
        outer = edges(*both(2 * blocks + odd_row), TL - 1, 0)
        inner = edges(*both(jnp.minimum(2 * i + 2, 2 * blocks - 1)), 0, 1)
        cells = jnp.where(i == last, below, tile(jnp.minimum((i + 1) * TL, blocks * TL - 1)))
        place(taps_ref, TL + 1, cells, jnp.where(i == last, outer, inner))
        for part in range(2):
            before, after = both(2 * i + part)
            merged = jnp.where(lanes % 2 == 1, after, pltpu.roll(before, 2, 1))
            for u in range(TL // 2):
                t = part * (TL // 2) + u
                place(taps_ref, t + 1, tile(i * TL + t), pltpu.roll(merged, TL - 2 - 2 * u, 1))

    def convolve(i, taps_ref, out_ref):
        pair = 2 * GROUP
        for k in range(TL // pair):
            base = k * pair * tap
            window = jnp.concatenate(
                [taps_ref[at : at + reach, :] for at in (base, base + GROUP * tap)], axis=1
            )
            out = jnp.dot(weight_ref[...], window, preferred_element_type=jnp.float32)
            out = out.reshape(channels, GROUP, 2 * TL)
            out = jnp.concatenate([out[:, :, :TL], out[:, :, TL:]], axis=1)
            rows = pl.ds(pl.multiple_of(i * TL + k * pair, pair), pair)
            out = out + plain_ref[:, rows, :].astype(jnp.float32)
            out_ref[:, k * pair : (k + 1) * pair, :] = out.astype(jnp.bfloat16)

    def flush(i, out_ref, slot):
        rows = pl.ds(pl.multiple_of(i * TL, TL), TL)
        return pltpu.make_async_copy(out_ref, texture_ref.at[:, rows, :], sems.at[slot])

    fill(0, even_ref)

    @pl.loop(0, blocks // 2)
    def _(h):
        @pl.when(h > 0)
        def _():
            flush(2 * h - 2, even_out_ref, 0).wait()

        fill(2 * h + 1, odd_ref)
        convolve(2 * h, even_ref, even_out_ref)
        flush(2 * h, even_out_ref, 0).start()

        @pl.when(h > 0)
        def _():
            flush(2 * h - 1, odd_out_ref, 1).wait()

        fill(jnp.minimum(2 * h + 2, blocks - 1), even_ref)
        convolve(2 * h + 1, odd_ref, odd_out_ref)
        flush(2 * h + 1, odd_out_ref, 1).start()

    flush(blocks - 2, even_out_ref, 0).wait()
    flush(blocks - 1, odd_out_ref, 1).wait()


def texture_call(place, joined, plain, *edges):
    channels = plain.shape[0]
    half = jnp.bfloat16
    taps = pltpu.VMEM(((TL + 2) * 3 * channels, TL), half)
    block = pltpu.VMEM((channels, TL, TL), half)
    return pl.pallas_call(
        texture_kernel,
        out_shape=jax.ShapeDtypeStruct(plain.shape, half),
        in_specs=[SCALARS] + [WHOLE] * (2 + len(edges)),
        out_specs=pl.BlockSpec(memory_space=pl.ANY),
        scratch_shapes=[taps, taps, block, block, pltpu.SemaphoreType.DMA((2,))],
        compiler_params=pltpu.CompilerParams(vmem_limit_bytes=VMEM_BYTES),
    )(place, joined, plain, *edges)


def local(
    image,
    conv_first,
    conv_second,
    conv_uv,
    send_block,
    send_shift,
    send_weight,
    send_count,
    recv_tile,
):
    half = jnp.bfloat16
    pixels = image[0]
    channels, strip_rows, width = pixels.shape
    place = jnp.stack(
        [lax.axis_index("row"), lax.axis_size("row"), lax.axis_index("cam")]
    ).astype(jnp.int32)
    odd = place[0] % 2 == 1
    head = pixels[:, :2].transpose(1, 0, 2)
    tail = pixels[:, -2:].transpose(1, 0, 2)
    near = swap(jnp.where(odd, head, tail), jnp.where(odd, tail, head), "row")
    peers, capacity = send_block.shape[2:]
    entries = peers * capacity
    message = channels * capacity + capacity // 2
    used = lax.broadcasted_iota(jnp.int32, (peers, capacity), 1) < send_count.reshape(peers, 1)
    slots = (
        send_block[0, 0]
        + (send_shift[0, 0] << SHIFT_BIT)
        + (jnp.where(used, send_weight[0, 0], 0) << WEIGHT_BIT)
    )
    tap = 3 * channels
    inner = strip_rows - GROUP
    bands = pltpu.VMEM((GROUP * channels, (GROUP + 2) * tap), half)
    strip = pl.pallas_call(
        strip_kernel,
        out_shape=(
            jax.ShapeDtypeStruct((strip_rows * tap, width), half),
            jax.ShapeDtypeStruct((inner * tap, width), half),
        ),
        in_specs=[WHOLE] * 2,
        out_specs=(WHOLE,) * 2,
        scratch_shapes=[
            pltpu.VMEM((width // TL, channels * (strip_rows + PAD), TL), jnp.float32),
            pltpu.VMEM((inner, channels, width), half),
            bands,
        ],
        compiler_params=pltpu.CompilerParams(vmem_limit_bytes=STRIP_BYTES),
        cost_estimate=pl.CostEstimate(
            flops=2 * (inner * channels) * (3 * tap) * width,
            bytes_accessed=4 * strip_rows * tap * width,
            transcendentals=inner * channels * width,
        ),
    )(pixels, conv_first)
    payload = pl.pallas_call(
        send_kernel,
        out_shape=pltpu.HBM((peers, message, TL), half),
        scratch_shapes=[
            pltpu.VMEM((4 * tap, width), half),
            bands,
            bands,
            pltpu.VMEM((GROUP + 2, channels, width), half),
            pltpu.VMEM(((GROUP + 2) * tap, width), half),
            pltpu.VMEM((strip_rows * width // TL, channels, TL), half),
            pltpu.VMEM((peers, message, TL), half),
            pltpu.SemaphoreType.DMA((8,)),
        ]
        + [pltpu.VMEM((channels * (capacity + PAD), TL), jnp.float32) for _ in range(4)],
        in_specs=[SCALARS] * 2 + [WHOLE] * 6,
        out_specs=pl.BlockSpec(memory_space=pl.ANY),
        compiler_params=pltpu.CompilerParams(vmem_limit_bytes=SEND_BYTES),
    )(place, slots, *strip, *near, conv_first, conv_second)
    arrived = lax.all_to_all(payload, ("cam", "row"), split_axis=0, concat_axis=0, tiled=True)
    joined, plain, edge, *ends = join_call(place, recv_tile.reshape(1, entries), arrived, channels)
    ends = swap(*ends, "row")
    rim = jnp.concatenate([edge, *ends], axis=1)
    rims = swap(rim, rim, "cam")
    return texture_call(place, joined, plain, *ends, *rims, band(conv_uv, True))


def solution(mesh):
    return jax.shard_map(
        local,
        mesh=mesh,
        in_specs=(
            P("cam", None, "row", None),
            P(),
            P(),
            P(),
            P("cam", "row", None, None),
            P("cam", "row", None, None),
            P("cam", "row", None, None),
            P("cam", "row", None),
            P("row", "cam", None, None),
        ),
        out_specs=P(None, "row", "cam"),
        check_vma=False,
    )
```
